32 devices in a mesh: user: 8 (over y, x, core), item: 4 (over z).
Axes of the slice: x: 2, y: 2, z: 4, core: 2. Of those that a mesh axis runs over, the one named last changes fastest.
Arguments:
- user_factors: float32 [4096, 256], P('user'), may hold values from -1.5 to 1.5
- item_factors: float32 [32768, 256], P(('user', 'item')), may hold values from -1.5 to 1.5
- feedback: bfloat16 [128, 4096, 128], P('item', 'user'), may hold values from 0 to 1
- item_pick: int32 [32, 32], replicated, may hold values from 0 to 7, as said below
- user_noise: float32 [4096, 256], P('user'), may hold values from -6 to 6
- item_noise: float32 [32768, 256], P(('user', 'item')), may hold values from -6 to 6
Outputs:
- new_user: float32 [4096, 256], P('user')
- new_item: float32 [32768, 256], P(('user', 'item'))
The draws below stay inside these ranges and needn't reach their ends.
Inputs may be any that keep to these rules, and one draw needn't show every extreme that they name: For every owner o and every user slab u, the 4 entries item_pick[u * 4 + i, o] are distinct, so that no tile appears twice.
All inputs are finite; a program needn't handle non-finite values.
Results may differ from the reference program's by a relative error of at most 0.00058.
Values may be sent and summed in bfloat16 or wider, within the bound.
A program may use at most 192 MiB of HBM per device.

```python
import math
import jax
import jax.numpy as jnp
from jax import lax

RANK = 256
TILE = 128
UB_DEV = 4
IB_DEV = 8
USERS = 4096
ITEMS = 32768
N_ITEM = 4
DEVICES = 32


def draw_item_pick(key, part):
    user_rows = DEVICES // N_ITEM
    ranking = jax.random.randint(key, (user_rows, DEVICES, IB_DEV), 0, 1 << 20) * IB_DEV + jnp.arange(IB_DEV, dtype=jnp.int32)
    picked = jnp.argsort(ranking, axis=-1)[:, :, :N_ITEM]
    return jnp.transpose(picked, (0, 2, 1)).reshape(DEVICES, DEVICES).astype(jnp.int32)


def level_of(own_key, dims, split, smallest, largest):
    def one(axis_at, shards_of):
        draws = jax.random.uniform(jax.random.fold_in(jax.random.fold_in(own_key, 6), axis_at), (shards_of,), jnp.float32, smallest / len(split), largest / len(split))
        return jnp.repeat(jnp.exp(draws), dims[axis_at] // shards_of).reshape((-1,) + (1,) * (len(dims) - axis_at - 1))

    factor_of = one(*split[0])
    for cut in split[1:]:
        factor_of = factor_of * one(*cut)
    return factor_of


def scatter_about(own_key, shape, deviation, reach, shards=(), kind=jnp.bfloat16):
    loudness = level_of(own_key, shape, shards, -0.22, 0.18) if shards else 1.0
    values = jax.random.normal(own_key, shape, jnp.float32) * deviation * loudness
    return jnp.minimum(jnp.maximum(values, -reach), reach).astype(kind)


def setup_inputs(seed: int = 0) -> dict:
    key_of = jax.random.split(jax.random.key(seed), 7)
    user_factors = scatter_about(key_of[0], (USERS, RANK), 0.25, 1.5, ((0, 8),), jnp.float32)
    item_factors = scatter_about(key_of[1], (ITEMS, RANK), 0.25, 1.5, ((0, 32),), jnp.float32)
    feedback = jnp.clip(1.0 * jax.random.uniform(key_of[2], (N_ITEM * DEVICES, USERS, TILE), jnp.float32) ** level_of(key_of[2], (N_ITEM * DEVICES, USERS, TILE), ((0, 4), (1, 8)), -0.2, 0.2), 0.0, 1.0).astype(jnp.bfloat16)
    item_pick = draw_item_pick(jax.random.fold_in(key_of[6], 71), 0)
    user_noise = scatter_about(key_of[4], (USERS, RANK), 1.0, 6.0, ((0, 8),), jnp.float32)
    item_noise = scatter_about(key_of[5], (ITEMS, RANK), 1.0, 6.0, ((0, 32),), jnp.float32)
    return {"user_factors": user_factors, "item_factors": item_factors, "feedback": feedback, "item_pick": item_pick, "user_noise": user_noise, "item_noise": item_noise}


step_size = 0.01
item_step = 0.1
prior_weight = 1.0
noise_scale = math.sqrt(0.02)
item_noise_scale = math.sqrt(0.2)

def reference(user_factors, item_factors, feedback, item_pick, user_noise, item_noise):
    slab_rows = UB_DEV * TILE
    item_half = item_factors.astype(jnp.bfloat16).reshape(IB_DEV * DEVICES, TILE, RANK)
    owners = jnp.arange(DEVICES, dtype=jnp.int32) * IB_DEV

    def one_device(totals, device):
        user_row = (device // N_ITEM).astype(jnp.int32)
        item_col = (device % N_ITEM).astype(jnp.int32)
        user_slab = lax.dynamic_slice_in_dim(user_factors, user_row * slab_rows, slab_rows, 0).astype(jnp.bfloat16)
        tiles = lax.dynamic_slice(feedback, (item_col * DEVICES, user_row * slab_rows, jnp.int32(0)), (DEVICES, slab_rows, TILE))
        blocks = (owners + item_pick[device]).astype(jnp.int32)
        fetched = item_half[blocks]
        scores = jnp.einsum('uk,ntk->nut', user_slab.astype(jnp.float32), fetched.astype(jnp.float32))
        residual = (jax.nn.sigmoid(scores) - tiles.astype(jnp.float32)).astype(jnp.bfloat16)
        user_grad = jnp.einsum('nut,ntk->uk', residual.astype(jnp.float32), fetched.astype(jnp.float32))
        item_part = jnp.einsum('nut,uk->ntk', residual.astype(jnp.float32), user_slab.astype(jnp.float32))
        totals = totals.at[blocks].add(item_part)
        return (totals, user_grad)
    start_grad = jnp.zeros((IB_DEV * DEVICES, TILE, RANK), jnp.float32)
    item_grad, user_parts = lax.scan(one_device, start_grad, jnp.arange(DEVICES, dtype=jnp.int32))
    user_grad = lax.optimization_barrier(jnp.sum(user_parts.reshape(DEVICES // N_ITEM, N_ITEM, slab_rows, RANK), axis=1)).reshape(USERS, RANK)
    new_user = user_factors - step_size * (user_grad + prior_weight * user_factors) + noise_scale * user_noise
    new_item = item_factors - item_step * (item_grad.reshape(ITEMS, RANK) + prior_weight * item_factors) + item_noise_scale * item_noise
    return (new_user, new_item)
```

```python
import functools
import math

import jax
import jax.numpy as jnp
from jax import lax
from jax.experimental import pallas as pl
from jax.experimental.pallas import tpu as pltpu
from jax.sharding import PartitionSpec as P

step_size = 0.01
item_step = 0.1
prior_weight = 1.0
noise_scale = math.sqrt(0.02)
item_noise_scale = math.sqrt(0.2)

FACTOR_BOUND = 1.5
LEVELS = 32766.0
HALVES = 2
RUN = 4
PAD = 8


def encode(ref, value, unit):
    rows = value.shape[0]
    largest = jnp.max(jnp.abs(value), axis=0, keepdims=True)
    count = jnp.floor(largest * (1.0 / (LEVELS * unit))) + 1.0
    inverse = 1.0 / (count * unit)
    ref[pl.ds(0, rows), :] = jnp.round(value * inverse).astype(jnp.int32).astype(jnp.int16)
    ref[pl.ds(rows, PAD), :] = jnp.broadcast_to(count, (PAD, value.shape[1])).astype(jnp.int32).astype(jnp.int16)


def decode(ref, weight, start=0, size=None):
    rows = ref.shape[0] - PAD
    size = rows if size is None else size
    count = ref[pl.ds(rows, PAD), :].astype(jnp.float32)[0:1]
    return ref[pl.ds(start, size), :].astype(jnp.float32) * (count * weight)


def kernel(
    U, Z, H, pick, items_wide, user_wide, feedback, item_out, user_out, *scratch
):
    held = scratch[:H]
    zbufs = scratch[H: H + 2 * (Z - 1) * H]
    (user, og, arr, gs, gr, cs, cr, crd, fb, us, ur, ugs, ugr, ug, values, sums, zsend, zrecv, isend, irecv, gsend,
     grecv, csend, crecv, cdrecv, fsem, usend, urecv, vsend, vrecv) = scratch[H + 2 * (Z - 1) * H:]
    B, T, K = items_wide.shape
    R = T // H
    N = user.shape[0]
    G = fb.shape[1]
    groups = U // G
    piece = N // Z
    runs = B // RUN
    me = lax.axis_index("user")
    z = lax.axis_index("item")
    item_unit = N * FACTOR_BOUND * U / LEVELS / 32000.0
    user_unit = U * Z * T * FACTOR_BOUND * Z / LEVELS / 32000.0

    def far(axis, to, src, dst, ssem, rsem):
        return pltpu.make_async_remote_copy(
            src_ref=src, dst_ref=dst, send_sem=ssem, recv_sem=rsem,
            device_id={axis: to}, device_id_type=pl.DeviceIdType.MESH)

    barrier = pltpu.get_barrier_semaphore()

    def greet_user(j, c):
        pl.semaphore_signal(barrier, inc=1, device_id={"user": lax.rem(me + j, U)}, device_id_type=pl.DeviceIdType.MESH)
        return c

    lax.fori_loop(1, U, greet_user, 0)
    for j in range(1, Z):
        pl.semaphore_signal(barrier, inc=1, device_id={"item": lax.rem(z + j, Z)}, device_id_type=pl.DeviceIdType.MESH)

    def rows_of(h):
        return pl.ds(pl.multiple_of(lax.rem(me + h, H) * R, R), R)

    for h in range(H):
        held[h][...] = items_wide[:, rows_of(h), :].astype(jnp.bfloat16)

    pl.semaphore_wait(barrier, U - 1 + Z - 1)

    def zbuf(d, way, h):
        return held[h] if d == 0 else zbufs[(2 * (d - 1) + way) * H + h]

    def zcopy(d, way, h):
        k = (2 * (d - 1) + way) * H + h
        return far("item", z + (1 if way == 0 else -1), zbuf(d - 1, way, h), zbuf(d, way, h), zsend.at[k], zrecv.at[k])

    def can_send(d, way):
        return (z - (d - 1) >= 0) & (z + 1 < Z) if way == 0 else (z + (d - 1) < Z) & (z >= 1)

    def comes(d, way):
        return z - d >= 0 if way == 0 else z + d < Z

    for h in range(H):
        for way in (0, 1):
            pl.when(can_send(1, way))(lambda way=way, h=h: zcopy(1, way, h).start())

    user[...] = user_wide[...].astype(jnp.bfloat16)

    def slot_of(o, h):
        return o // H * H + lax.rem(o + h, H)

    def owner_of(j, h):
        return j // H * H + lax.rem(j + H - h, H)

    def icopy(p, h, to, src):
        return far("user", to, og.at[p, h, to], arr.at[p, h, slot_of(src, h)], isend.at[p, h, to], irecv.at[p, h, src])

    def spread(p, h, blocks):
        def one(j, c):
            to = lax.rem(me + j, U)
            og[p, h, to] = blocks[pick[to * Z + z, me * Z + p]]
            icopy(p, h, to, me).start()
            return c
        lax.fori_loop(1, U, one, 0)
        arr[p, h, slot_of(me, h)] = blocks[pick[me * Z + z, me * Z + p]]

    def gcopy(p, h, to, src):
        return far("user", to, gs.at[p, h, to], gr.at[p, h, src], gsend.at[p, h, to], grecv.at[p, h, src])

    def fcopy(p, g, at):
        return pltpu.make_async_copy(feedback.at[pl.ds(G * g, G), p], fb.at[at], fsem.at[at])

    lane = lax.broadcasted_iota(jnp.int32, (N, T), 1)

    def group_of(j):
        return lax.rem(me // G + groups - j, groups)

    def compute(p, h, send):
        fcopy(p, group_of(0), 0).start()

        def one(j, c):
            g = group_of(j)
            at = lax.rem(j, 2)

            @pl.when(j + 1 < groups)
            def _():
                fcopy(p, group_of(j + 1), 1 - at).start()

            def arrive(t, c):
                o = G * g + t
                pl.when(o != me)(lambda: icopy(p, h, me, o).wait_recv())
                return c

            lax.fori_loop(0, G, arrive, 0)
            fcopy(p, g, at).wait()
            tile = arr[p, h, pl.ds(G * g, G)].reshape(G * R, K)
            scores = lax.dot_general(user[...], tile, (((1,), (1,)), ((), ())), preferred_element_type=jnp.float32)
            target = []
            for m in range(G // H):
                lanes = fb[at, m * H + owner_of(H - 1, h)]
                for s in range(H - 1):
                    lanes = jnp.where((lane >= s * R) & (lane < (s + 1) * R), fb[at, m * H + owner_of(s, h)], lanes)
                target.append(lanes)
            target = jnp.concatenate(target, axis=1).astype(jnp.float32)
            residual = (0.5 * jnp.tanh(0.5 * scores) + (0.5 - target)).astype(jnp.bfloat16)
            part = lax.dot_general(residual, user[...], (((0,), (0,)), ((), ())), preferred_element_type=jnp.float32)
            for t in range(G):
                o = owner_of(G * g + t, h)
                encode(gs.at[p, h, o], part[t * R:(t + 1) * R], item_unit)

                @pl.when(o == me)
                def _():
                    gr[p, h, me] = gs[p, h, me]

                if send:
                    pl.when(o != me)(lambda: gcopy(p, h, o, me).start())
            ug[...] += jnp.dot(residual, tile, preferred_element_type=jnp.float32)
            return c

        lax.fori_loop(0, groups, one, 0)

    def collect(p, h, way):
        def one(j, c):
            u = lax.rem(me + j, U)
            pl.when(j > 0)(lambda: gcopy(p, h, me, u).wait_recv())
            values[way, u] = decode(gr.at[p, h, u], item_unit)
            return c
        lax.fori_loop(0, U, one, 0)

    def dense(p, b, way):
        def one(u, acc):
            weight = jnp.where(pick[u * Z + z, me * Z + p] == b, 1.0, 0.0).astype(jnp.float32)
            return acc + values[way, u] * weight
        return lax.fori_loop(0, U, one, jnp.zeros((R, K), jnp.float32), unroll=8)

    def up_copy(to, p, h, c):
        return far("item", to, cs.at[p, h, c], cr.at[p, h, c], csend.at[p, h, c], crecv.at[p, h, c])

    def last_copy(to, p, h, c):
        return far("item", to, cs.at[p, h, c], crd.at[h, c], csend.at[p, h, c], cdrecv.at[h, c])

    def phase(r, h):
        def target(way):
            return r + way * (Z - 1 - 2 * r)

        def active(way):
            return (way == 0) & (z < r) | (way == 1) & (z > Z - 1 - r)

        def source(way):
            return (way == 0) & (z == 0) | (way == 1) & (z == Z - 1)

        for way in (0, 1):
            pl.when(active(way))(lambda way=way: collect(target(way), h, way))

        def pass_on(c, way):
            p = target(way)
            to = z + 1 - 2 * way
            relay = jnp.logical_not(source(way))
            pl.when(relay)(lambda: up_copy(z, p, h, c).wait_recv())

            def one(i, carry):
                at = pl.ds(pl.multiple_of(i * R, R), R)
                sums[at, :] = dense(p, c * RUN + i, way)

                @pl.when(relay)
                def _():
                    sums[at, :] += decode(cr.at[p, h, c], item_unit, pl.multiple_of(i * R, R), R)
                return carry
            lax.fori_loop(0, RUN, one, 0)
            encode(cs.at[p, h, c], sums[...], item_unit)
            last = (way == 1) & (to == p)
            pl.when(last)(lambda: last_copy(to, p, h, c).start())
            pl.when(jnp.logical_not(last))(lambda: up_copy(to, p, h, c).start())

        def one(k, carry):
            c = k // 2
            low = jnp.where(2 * z < Z - 1, 1, 0)
            way = lax.rem(k + 1 - low, 2)
            pl.when(active(way))(lambda: pass_on(c, way))
            return carry
        lax.fori_loop(0, 2 * runs, one, 0)

    def ucopy(to, src):
        return far("item", to, us.at[to], ur.at[src], usend.at[to], urecv.at[src])

    def plane(d, way):
        return z - d if way == 0 else z + d

    def own_out():
        for h in range(H):
            def one(j, c):
                gcopy(z, h, lax.rem(me + j, U), me).start()
                return c
            lax.fori_loop(1, U, one, 0)
        for j in range(1, Z):
            to = lax.rem(z + j, Z)
            encode(us.at[to], ug[pl.ds(pl.multiple_of(to * piece, piece), piece), :], user_unit)
            ucopy(to, z).start()

    with jax.named_scope("spread_own"):
        for h in range(H):
            spread(z, h, held[h])
    ug[...] = jnp.zeros_like(ug)

    with jax.named_scope("compute_own"):
        def own(h, c):
            compute(z, h, False)
            return c
        lax.fori_loop(0, H, own, 0)

    farthest = jnp.maximum(z, Z - 1 - z)

    def step(s, carry):
        d = s // H + 1
        h = lax.rem(s, H)
        with jax.named_scope("arrive"):
            for e in range(1, Z):
                for way in (0, 1):
                    for f in range(H):
                        @pl.when(comes(e, way) & (s == (e - 1) * H + f))
                        def _(e=e, way=way, f=f):
                            zcopy(e, way, f).wait_recv()
                            if e + 1 < Z:
                                pl.when(can_send(e + 1, way))(lambda: zcopy(e + 1, way, f).start())
                            spread(plane(e, way), f, zbuf(e, way, f))
        with jax.named_scope("compute"):
            for way in (0, 1):
                pl.when(comes(d, way))(lambda way=way: compute(plane(d, way), h, True))
        with jax.named_scope("own_out"):
            pl.when((d == farthest) & (h == H - 1))(own_out)
        with jax.named_scope("phase"):
            pl.when(s > 0)(lambda: phase((s - 1) // H + 1, lax.rem(s - 1, H)))
        return carry

    steps = (Z - 1) * H
    lax.fori_loop(0, steps, step, 0)
    with jax.named_scope("lastphase"):
        phase(Z - 1, H - 1)

    def vcopy(to, src, j):
        return far("item", to, ugs, ugr.at[src], vsend.at[j], vrecv.at[src])

    def share_users():
        total = ug[pl.ds(pl.multiple_of(z * piece, piece), piece), :]
        for j in range(1, Z):
            src = lax.rem(z + j, Z)
            ucopy(z, src).wait_recv()
            total = total + decode(ur.at[src], user_unit)
        encode(ugs, total, user_unit)
        for j in range(1, Z):
            vcopy(lax.rem(z + j, Z), z, j - 1).start()
        user_out[pl.ds(pl.multiple_of(z * piece, piece), piece), :] = decode(ugs, user_unit)

    with jax.named_scope("share"):
        share_users()

    def finish(h, carry):
        collect(z, h, 0)
        rows = rows_of(h)

        def one(b, carry):
            c = b // RUN
            at = pl.multiple_of(lax.rem(b, RUN) * R, R)
            item_out[b, rows, :] = dense(z, b, 0)

            @pl.when(z > 0)
            def _():
                pl.when(lax.rem(b, RUN) == 0)(lambda: up_copy(z, z, h, c).wait_recv())
                item_out[b, rows, :] += decode(cr.at[z, h, c], item_unit, at, R)

            @pl.when(z < Z - 1)
            def _():
                pl.when(lax.rem(b, RUN) == 0)(lambda: last_copy(z, z, h, c).wait_recv())
                item_out[b, rows, :] += decode(crd.at[h, c], item_unit, at, R)
            return carry

        lax.fori_loop(0, B, one, 0)
        return carry

    with jax.named_scope("finish"):
        lax.fori_loop(0, H, finish, 0)

    with jax.named_scope("userout"):
        for j in range(1, Z):
            src = lax.rem(z + j, Z)
            vcopy(z, src, j - 1).wait_recv()
            user_out[pl.ds(pl.multiple_of(src * piece, piece), piece), :] = decode(ugr.at[src], user_unit)

    for d in range(1, Z):
        for way in (0, 1):
            for h in range(H):
                pl.when(can_send(d, way))(lambda d=d, way=way, h=h: zcopy(d, way, h).wait_send())

    def drain(j, c):
        to = lax.rem(me + j, U)

        def one(k, c):
            icopy(k // H, lax.rem(k, H), to, me).wait_send()
            gcopy(k // H, lax.rem(k, H), to, me).wait_send()
            return c
        return lax.fori_loop(0, Z * H, one, c)

    lax.fori_loop(1, U, drain, 0)
    for j in range(1, Z):
        to = lax.rem(z + j, Z)
        ucopy(to, z).wait_send()
        vcopy(to, z, j - 1).wait_send()

        def drained(k, c):
            up_copy(z, to, k // runs, lax.rem(k, runs)).wait_send()
            return c
        lax.fori_loop(0, H * runs, drained, 0)


def exchange(pick, items, user, feedback, U, Z):
    B, T, K = items.shape
    N = user.shape[0]
    H = HALVES
    R = T // H
    G = min(U, 2 * H)
    piece = N // Z
    runs = B // RUN
    dma = pltpu.SemaphoreType.DMA
    i16 = jnp.int16
    bf16 = jnp.bfloat16
    vmem = pl.BlockSpec(memory_space=pltpu.VMEM)
    return pl.pallas_call(
        functools.partial(kernel, U, Z, H),
        out_shape=(jax.ShapeDtypeStruct((B, T, K), jnp.float32), jax.ShapeDtypeStruct((N, K), jnp.float32)),
        in_specs=[pl.BlockSpec(memory_space=pltpu.SMEM), vmem, vmem, pl.BlockSpec(memory_space=pl.ANY)],
        out_specs=(vmem, vmem),
        scratch_shapes=[pltpu.VMEM((B, R, K), bf16)] * (H * (2 * (Z - 1) + 1)) + [
            pltpu.VMEM((N, K), bf16),
            pltpu.VMEM((Z, H, U, R, K), bf16),
            pltpu.VMEM((Z, H, U, R, K), bf16),
            pltpu.VMEM((Z, H, U, R + PAD, K), i16),
            pltpu.VMEM((Z, H, U, R + PAD, K), i16),
            pltpu.VMEM((Z, H, runs, RUN * R + PAD, K), i16),
            pltpu.VMEM((Z, H, runs, RUN * R + PAD, K), i16),
            pltpu.VMEM((H, runs, RUN * R + PAD, K), i16),
            pltpu.VMEM((2, G, N, T), bf16),
            pltpu.VMEM((Z, piece + PAD, K), i16),
            pltpu.VMEM((Z, piece + PAD, K), i16),
            pltpu.VMEM((piece + PAD, K), i16),
            pltpu.VMEM((Z, piece + PAD, K), i16),
            pltpu.VMEM((N, K), jnp.float32),
            pltpu.VMEM((2, U, R, K), jnp.float32),
            pltpu.VMEM((RUN * R, K), jnp.float32),
            dma((2 * (Z - 1) * H,)), dma((2 * (Z - 1) * H,)),
            dma((Z, H, U)), dma((Z, H, U)), dma((Z, H, U)), dma((Z, H, U)),
            dma((Z, H, runs)), dma((Z, H, runs)), dma((H, runs)),
            dma((2,)),
            dma((Z,)), dma((Z,)), dma((Z,)), dma((Z,)),
        ],
        compiler_params=pltpu.CompilerParams(
            collective_id=0, has_side_effects=True, vmem_limit_bytes=63 * 2**20),
    )(pick, items, user, feedback)


def local(user_factors, item_factors, feedback, item_pick, user_noise, item_noise):
    U, Z = lax.axis_size("user"), lax.axis_size("item")
    tile, rank = feedback.shape[2], item_factors.shape[1]
    held = item_factors.shape[0] // tile
    items = item_factors.reshape(held, tile, rank)
    item_grad, user_grad = exchange(
        item_pick, items, user_factors,
        feedback.reshape(U, Z, feedback.shape[1], tile), U, Z)
    item_grad = item_grad.reshape(item_factors.shape)
    new_item = item_factors - item_step * (item_grad + prior_weight * item_factors) + item_noise_scale * item_noise
    new_user = user_factors - step_size * (user_grad + prior_weight * user_factors) + noise_scale * user_noise
    return (new_user, new_item)


def solution(mesh):
    in_specs = (
        P("user", None),
        P(("user", "item"), None),
        P("item", "user", None),
        P(),
        P("user", None),
        P(("user", "item"), None),
    )
    out_specs = (P("user", None), P(("user", "item"), None))
    return jax.shard_map(local, mesh=mesh, in_specs=in_specs, out_specs=out_specs, check_vma=False)
```

```python
import functools
import math

import jax
import jax.numpy as jnp
from jax import lax
from jax.experimental import pallas as pl
from jax.experimental.pallas import tpu as pltpu
from jax.sharding import PartitionSpec as P

step_size = 0.01
item_step = 0.1
prior_weight = 1.0
noise_scale = math.sqrt(0.02)
item_noise_scale = math.sqrt(0.2)

FACTOR_BOUND = 1.5
LEVELS = 32766.0
HALVES = 2
RUN = 4
PAD = 8
PIECES = 4


def encode(ref, value, unit):
    rows = value.shape[0]
    largest = jnp.max(jnp.abs(value), axis=0, keepdims=True)
    count = jnp.floor(largest * (1.0 / (LEVELS * unit))) + 1.0
    inverse = 1.0 / (count * unit)
    ref[pl.ds(0, rows), :] = jnp.round(value * inverse).astype(jnp.int32).astype(jnp.int16)
    ref[pl.ds(rows, PAD), :] = jnp.broadcast_to(count, (PAD, value.shape[1])).astype(jnp.int32).astype(jnp.int16)


def decode(ref, weight, start=0, size=None):
    rows = ref.shape[0] - PAD
    size = rows if size is None else size
    count = ref[pl.ds(rows, PAD), :].astype(jnp.float32)[0:1]
    return ref[pl.ds(start, size), :].astype(jnp.float32) * (count * weight)


def kernel(
    U, Z, H, pick, items_wide, user_wide, feedback, item_out, user_out, *scratch
):
    held = scratch[:H]
    zbufs = scratch[H: H + 2 * (Z - 1) * H]
    (user, og, arr, gs, gr, cs, cr, crd, fb, us, ur, xr, ws, wr, ug, values, sums, zsend, zrecv, isend, irecv, gsend,
     grecv, csend, crecv, cdrecv, fsem, usend, urecv, xrecv, wsend, wrecv) = scratch[H + 2 * (Z - 1) * H:]
    B, T, K = items_wide.shape
    R = T // H
    N = user.shape[0]
    G = fb.shape[1]
    groups = U // G
    piece = N // PIECES
    runs = B // RUN
    me = lax.axis_index("user")
    z = lax.axis_index("item")
    item_unit = N * FACTOR_BOUND * U / LEVELS / 32000.0
    user_unit = U * Z * T * FACTOR_BOUND * Z / LEVELS / 32000.0

    def far(axis, to, src, dst, ssem, rsem):
        return pltpu.make_async_remote_copy(
            src_ref=src, dst_ref=dst, send_sem=ssem, recv_sem=rsem,
            device_id={axis: to}, device_id_type=pl.DeviceIdType.MESH)

    barrier = pltpu.get_barrier_semaphore()

    def greet_user(j, c):
        pl.semaphore_signal(barrier, inc=1, device_id={"user": lax.rem(me + j, U)}, device_id_type=pl.DeviceIdType.MESH)
        return c

    lax.fori_loop(1, U, greet_user, 0)
    for j in range(1, Z):
        pl.semaphore_signal(barrier, inc=1, device_id={"item": lax.rem(z + j, Z)}, device_id_type=pl.DeviceIdType.MESH)

    def rows_of(h):
        return pl.ds(pl.multiple_of(lax.rem(me + h, H) * R, R), R)

    for h in range(H):
        held[h][...] = items_wide[:, rows_of(h), :].astype(jnp.bfloat16)

    pl.semaphore_wait(barrier, U - 1 + Z - 1)

    def zbuf(d, way, h):
        return held[h] if d == 0 else zbufs[(2 * (d - 1) + way) * H + h]

    def zcopy(d, way, h):
        k = (2 * (d - 1) + way) * H + h
        return far("item", z + (1 if way == 0 else -1), zbuf(d - 1, way, h), zbuf(d, way, h), zsend.at[k], zrecv.at[k])

    def can_send(d, way):
        return (z - (d - 1) >= 0) & (z + 1 < Z) if way == 0 else (z + (d - 1) < Z) & (z >= 1)

    def comes(d, way):
        return z - d >= 0 if way == 0 else z + d < Z

    for h in range(H):
        for way in (0, 1):
            pl.when(can_send(1, way))(lambda way=way, h=h: zcopy(1, way, h).start())

    user[...] = user_wide[...].astype(jnp.bfloat16)

    def slot_of(o, h):
        return o // H * H + lax.rem(o + h, H)

    def owner_of(j, h):
        return j // H * H + lax.rem(j + H - h, H)

    def icopy(p, h, to, src):
        return far("user", to, og.at[p, h, to], arr.at[p, h, slot_of(src, h)], isend.at[p, h, to], irecv.at[p, h, src])

    def spread(p, h, blocks):
        def one(j, c):
            to = lax.rem(me + j, U)
            og[p, h, to] = blocks[pick[to * Z + z, me * Z + p]]
            icopy(p, h, to, me).start()
            return c
        lax.fori_loop(1, U, one, 0)
        arr[p, h, slot_of(me, h)] = blocks[pick[me * Z + z, me * Z + p]]

    def gcopy(p, h, to, src):
        return far("user", to, gs.at[p, h, to], gr.at[p, h, src], gsend.at[p, h, to], grecv.at[p, h, src])

    def fcopy(p, g, at):
        return pltpu.make_async_copy(feedback.at[pl.ds(G * g, G), p], fb.at[at], fsem.at[at])

    lane = lax.broadcasted_iota(jnp.int32, (N, T), 1)

    def group_of(j):
        return lax.rem(me // G + groups - j, groups)

    def prefetch(p, way):
        for j in range(min(2, groups)):
            fcopy(p, group_of(j), 2 * way + j).start()

    def compute(p, h, way, send):
        def one(j, c):
            g = group_of(j)
            at = 2 * way + lax.rem(j, 2)

            def arrive(t, c):
                o = G * g + t
                pl.when(o != me)(lambda: icopy(p, h, me, o).wait_recv())
                return c

            lax.fori_loop(0, G, arrive, 0)
            fcopy(p, g, at).wait()
            tile = arr[p, h, pl.ds(G * g, G)].reshape(G * R, K)
            scores = lax.dot_general(user[...], tile, (((1,), (1,)), ((), ())), preferred_element_type=jnp.float32)
            target = []
            for m in range(G // H):
                lanes = fb[at, m * H + owner_of(H - 1, h)]
                for s in range(H - 1):
                    lanes = jnp.where((lane >= s * R) & (lane < (s + 1) * R), fb[at, m * H + owner_of(s, h)], lanes)
                target.append(lanes)
            target = jnp.concatenate(target, axis=1).astype(jnp.float32)
            residual = (0.5 * jnp.tanh(0.5 * scores) + (0.5 - target)).astype(jnp.bfloat16)
            part = lax.dot_general(residual, user[...], (((0,), (0,)), ((), ())), preferred_element_type=jnp.float32)
            for t in range(G):
                o = owner_of(G * g + t, h)
                encode(gs.at[p, h, o], part[t * R:(t + 1) * R], item_unit)

                @pl.when(o == me)
                def _():
                    gr[p, h, me] = gs[p, h, me]

                if send:
                    pl.when(o != me)(lambda: gcopy(p, h, o, me).start())
            ug[...] += jnp.dot(residual, tile, preferred_element_type=jnp.float32)
            pl.when(j + 2 < groups)(lambda: fcopy(p, group_of(j + 2), at).start())
            return c

        lax.fori_loop(0, groups, one, 0)

    def collect(p, h, way):
        def one(j, c):
            u = lax.rem(me + j, U)
            pl.when(j > 0)(lambda: gcopy(p, h, me, u).wait_recv())
            values[way, u] = decode(gr.at[p, h, u], item_unit)
            return c
        lax.fori_loop(0, U, one, 0)

    def dense(p, b, way):
        def one(u, acc):
            weight = jnp.where(pick[u * Z + z, me * Z + p] == b, 1.0, 0.0).astype(jnp.float32)
            return acc + values[way, u] * weight
        return lax.fori_loop(0, U, one, jnp.zeros((R, K), jnp.float32), unroll=8)

    def up_copy(to, p, h, c):
        return far("item", to, cs.at[p, h, c], cr.at[p, h, c], csend.at[p, h, c], crecv.at[p, h, c])

    def last_copy(to, p, h, c):
        return far("item", to, cs.at[p, h, c], crd.at[h, c], csend.at[p, h, c], cdrecv.at[h, c])

    def phase(r, h, begin, end):
        def target(way):
            return r + way * (Z - 1 - 2 * r)

        def active(way):
            return (way == 0) & (z < r) | (way == 1) & (z > Z - 1 - r)

        def source(way):
            return (way == 0) & (z == 0) | (way == 1) & (z == Z - 1)

        def in_turn(k):
            return lax.rem(k + jnp.where(2 * z < Z - 1, 0, 1), 2)

        def gather(k, carry):
            way = in_turn(k)
            pl.when(active(way))(lambda: collect(target(way), h, way))
            return carry
        lax.fori_loop(begin, end, gather, 0)

        def pass_on(c, way):
            p = target(way)
            to = z + 1 - 2 * way
            relay = jnp.logical_not(source(way))
            pl.when(relay)(lambda: up_copy(z, p, h, c).wait_recv())

            def one(i, carry):
                at = pl.ds(pl.multiple_of(i * R, R), R)
                sums[at, :] = dense(p, c * RUN + i, way)

                @pl.when(relay)
                def _():
                    sums[at, :] += decode(cr.at[p, h, c], item_unit, pl.multiple_of(i * R, R), R)
                return carry
            lax.fori_loop(0, RUN, one, 0)
            encode(cs.at[p, h, c], sums[...], item_unit)
            last = (way == 1) & (to == p)
            pl.when(last)(lambda: last_copy(to, p, h, c).start())
            pl.when(jnp.logical_not(last))(lambda: up_copy(to, p, h, c).start())

        def one(k, carry):
            way = in_turn(k // runs)
            pl.when(active(way))(lambda: pass_on(lax.rem(k, runs), way))
            return carry
        lax.fori_loop(begin * runs, end * runs, one, 0)

    def plane(d, way):
        return z - d if way == 0 else z + d

    def own_out():
        for h in range(H):
            def one(j, c):
                gcopy(z, h, lax.rem(me + j, U), me).start()
                return c
            lax.fori_loop(1, U, one, 0)

    def arrive(s):
        for e in range(1, Z):
            for way in (0, 1):
                for f in range(H):
                    @pl.when(comes(e, way) & (s == (e - 1) * H + f))
                    def _(e=e, way=way, f=f):
                        zcopy(e, way, f).wait_recv()
                        if e + 1 < Z:
                            pl.when(can_send(e + 1, way))(lambda: zcopy(e + 1, way, f).start())
                        spread(plane(e, way), f, zbuf(e, way, f))

    with jax.named_scope("spread_own"):
        for h in range(H):
            spread(z, h, held[h])
    ug[...] = jnp.zeros_like(ug)

    with jax.named_scope("compute_own"):
        def own(h, c):
            prefetch(z, 0)
            compute(z, h, 0, False)
            pl.when(h == 0)(lambda: arrive(h))
            return c
        lax.fori_loop(0, H, own, 0)

    edge = (z == 0) | (z == Z - 1)
    farthest = jnp.maximum(z, Z - 1 - z)
    steps = (Z - 1) * H

    def step(s, carry):
        d = s // H + 1
        h = lax.rem(s, H)
        for way in (0, 1):
            pl.when(comes(d, way))(lambda way=way: prefetch(plane(d, way), way))
        with jax.named_scope("arrive"):
            arrive(s + 1)
        with jax.named_scope("compute"):
            for way in (0, 1):
                pl.when(comes(d, way))(lambda way=way: compute(plane(d, way), h, way, True))
        with jax.named_scope("own_out"):
            pl.when(jnp.logical_not(edge) & (d == farthest) & (h == H - 1))(own_out)
        with jax.named_scope("phase"):
            ready = s - jnp.where(edge, 1, 0)
            pl.when((ready >= 0) & (ready < (Z - 2) * H))(lambda: phase(ready // H + 1, lax.rem(ready, H), 0, 2))
        return carry

    lax.fori_loop(0, steps, step, 0)

    half = Z // 2
    inward = jnp.where(z < half, 1, -1)
    middle = (z == half - 1) | (z == half)

    def in_copy(to, q):
        return far("item", to, us.at[q], ur.at[q], usend.at[q], urecv.at[q])

    def cross_copy(to, q):
        return far("item", to, us.at[q], xr.at[q], usend.at[q], xrecv.at[q])

    def out_copy(src, to, q):
        return far("item", to, src.at[q], wr.at[q], wsend.at[q], wrecv.at[q])

    def rows_q(q):
        return pl.ds(pl.multiple_of(q * piece, piece), piece)

    def users_in(q, carry):
        rows = rows_q(q)

        @pl.when(jnp.logical_not(edge))
        def _():
            in_copy(z, q).wait_recv()
            ug[rows, :] += decode(ur.at[q], user_unit)
        encode(us.at[q], ug[rows, :], user_unit)
        pl.when(middle)(lambda: cross_copy(z + inward, q).start())
        pl.when(jnp.logical_not(middle))(lambda: in_copy(z + inward, q).start())
        return carry

    def users_out(q, carry):
        rows = rows_q(q)

        @pl.when(middle)
        def _():
            cross_copy(z, q).wait_recv()
            encode(ws.at[q], decode(us.at[q], user_unit) + decode(xr.at[q], user_unit), user_unit)
            pl.when(jnp.logical_not(edge))(lambda: out_copy(ws, z - inward, q).start())
            user_out[rows, :] = decode(ws.at[q], user_unit)

        @pl.when(jnp.logical_not(middle))
        def _():
            out_copy(ws, z, q).wait_recv()
            pl.when(jnp.logical_not(edge))(lambda: out_copy(wr, z - inward, q).start())
            user_out[rows, :] = decode(wr.at[q], user_unit)
        return carry

    def users_back():
        lax.fori_loop(0, PIECES, users_out, 0)

    def last_phase(first, last, k):
        def one(h, c):
            phase(Z - 1, h, k, k + 1)
            return c
        lax.fori_loop(first, last, one, 0)

    with jax.named_scope("users_in"):
        lax.fori_loop(0, PIECES, users_in, 0)
    with jax.named_scope("phase_a"):
        last_phase(0, H - 1, 0)
    with jax.named_scope("users_mid"):
        pl.when(middle)(users_back)
    with jax.named_scope("phase_b"):
        last_phase(0, H - 1, 1)
    with jax.named_scope("phase_c"):
        last_phase(H - 1, H, 0)
    pl.when(edge)(own_out)
    with jax.named_scope("phase_d"):
        last_phase(H - 1, H, 1)

    def finish(h, carry):
        collect(z, h, 0)
        rows = rows_of(h)

        def one(b, carry):
            c = b // RUN
            at = pl.multiple_of(lax.rem(b, RUN) * R, R)
            item_out[b, rows, :] = dense(z, b, 0)

            @pl.when(z > 0)
            def _():
                pl.when(lax.rem(b, RUN) == 0)(lambda: up_copy(z, z, h, c).wait_recv())
                item_out[b, rows, :] += decode(cr.at[z, h, c], item_unit, at, R)

            @pl.when(z < Z - 1)
            def _():
                pl.when(lax.rem(b, RUN) == 0)(lambda: last_copy(z, z, h, c).wait_recv())
                item_out[b, rows, :] += decode(crd.at[h, c], item_unit, at, R)
            return carry

        lax.fori_loop(0, B, one, 0)
        return carry

    with jax.named_scope("finish"):
        lax.fori_loop(0, H, finish, 0)

    with jax.named_scope("userout"):
        pl.when(jnp.logical_not(middle))(users_back)

    for d in range(1, Z):
        for way in (0, 1):
            for h in range(H):
                pl.when(can_send(d, way))(lambda d=d, way=way, h=h: zcopy(d, way, h).wait_send())

    def drain(j, c):
        to = lax.rem(me + j, U)

        def one(k, c):
            icopy(k // H, lax.rem(k, H), to, me).wait_send()
            gcopy(k // H, lax.rem(k, H), to, me).wait_send()
            return c
        return lax.fori_loop(0, Z * H, one, c)

    lax.fori_loop(1, U, drain, 0)
    for j in range(1, Z):
        to = lax.rem(z + j, Z)
        def drained(k, c):
            up_copy(z, to, k // runs, lax.rem(k, runs)).wait_send()
            return c
        lax.fori_loop(0, H * runs, drained, 0)
    for q in range(PIECES):
        in_copy(z + inward, q).wait_send()
        pl.when(jnp.logical_not(edge))(lambda q=q: out_copy(ws, z - inward, q).wait_send())


def exchange(pick, items, user, feedback, U, Z):
    B, T, K = items.shape
    N = user.shape[0]
    H = HALVES
    R = T // H
    G = min(U, 2 * H)
    piece = N // PIECES
    runs = B // RUN
    dma = pltpu.SemaphoreType.DMA
    i16 = jnp.int16
    bf16 = jnp.bfloat16
    vmem = pl.BlockSpec(memory_space=pltpu.VMEM)
    return pl.pallas_call(
        functools.partial(kernel, U, Z, H),
        out_shape=(jax.ShapeDtypeStruct((B, T, K), jnp.float32), jax.ShapeDtypeStruct((N, K), jnp.float32)),
        in_specs=[pl.BlockSpec(memory_space=pltpu.SMEM), vmem, vmem, pl.BlockSpec(memory_space=pl.ANY)],
        out_specs=(vmem, vmem),
        scratch_shapes=[pltpu.VMEM((B, R, K), bf16)] * (H * (2 * (Z - 1) + 1)) + [
            pltpu.VMEM((N, K), bf16),
            pltpu.VMEM((Z, H, U, R, K), bf16),
            pltpu.VMEM((Z, H, U, R, K), bf16),
            pltpu.VMEM((Z, H, U, R + PAD, K), i16),
            pltpu.VMEM((Z, H, U, R + PAD, K), i16),
            pltpu.VMEM((Z, H, runs, RUN * R + PAD, K), i16),
            pltpu.VMEM((Z, H, runs, RUN * R + PAD, K), i16),
            pltpu.VMEM((H, runs, RUN * R + PAD, K), i16),
            pltpu.VMEM((4, G, N, T), bf16),
        ] + [pltpu.VMEM((PIECES, piece + PAD, K), i16)] * 5 + [
            pltpu.VMEM((N, K), jnp.float32),
            pltpu.VMEM((2, U, R, K), jnp.float32),
            pltpu.VMEM((RUN * R, K), jnp.float32),
            dma((2 * (Z - 1) * H,)), dma((2 * (Z - 1) * H,)),
            dma((Z, H, U)), dma((Z, H, U)), dma((Z, H, U)), dma((Z, H, U)),
            dma((Z, H, runs)), dma((Z, H, runs)), dma((H, runs)),
            dma((4,)),
            dma((PIECES,)), dma((PIECES,)), dma((PIECES,)), dma((PIECES,)), dma((PIECES,)),
        ],
        compiler_params=pltpu.CompilerParams(
            collective_id=0, has_side_effects=True, vmem_limit_bytes=63 * 2**20),
    )(pick, items, user, feedback)


def local(user_factors, item_factors, feedback, item_pick, user_noise, item_noise):
    U, Z = lax.axis_size("user"), lax.axis_size("item")
    tile, rank = feedback.shape[2], item_factors.shape[1]
    held = item_factors.shape[0] // tile
    items = item_factors.reshape(held, tile, rank)
    item_grad, user_grad = exchange(
        item_pick, items, user_factors,
        feedback.reshape(U, Z, feedback.shape[1], tile), U, Z)
    item_grad = item_grad.reshape(item_factors.shape)
    new_item = item_factors - item_step * (item_grad + prior_weight * item_factors) + item_noise_scale * item_noise
    new_user = user_factors - step_size * (user_grad + prior_weight * user_factors) + noise_scale * user_noise
    return (new_user, new_item)


def solution(mesh):
    in_specs = (
        P("user", None),
        P(("user", "item"), None),
        P("item", "user", None),
        P(),
        P("user", None),
        P(("user", "item"), None),
    )
    out_specs = (P("user", None), P(("user", "item"), None))
    return jax.shard_map(local, mesh=mesh, in_specs=in_specs, out_specs=out_specs, check_vma=False)
```

```python
import functools
import math

import jax
import jax.numpy as jnp
from jax import lax
from jax.experimental import pallas as pl
from jax.experimental.pallas import tpu as pltpu
from jax.sharding import PartitionSpec as P

step_size = 0.01
item_step = 0.1
prior_weight = 1.0
noise_scale = math.sqrt(0.02)
item_noise_scale = math.sqrt(0.2)

FACTOR_BOUND = 1.5
LEVELS = 32766.0
HALVES = 2
RUN = 4
PAD = 8
PIECES = 4


def encode(ref, value, unit):
    rows = value.shape[0]
    largest = jnp.max(jnp.abs(value), axis=0, keepdims=True)
    count = jnp.floor(largest * (1.0 / (LEVELS * unit))) + 1.0
    inverse = 1.0 / (count * unit)
    ref[pl.ds(0, rows), :] = jnp.round(value * inverse).astype(jnp.int32).astype(jnp.int16)
    ref[pl.ds(rows, PAD), :] = jnp.broadcast_to(count, (PAD, value.shape[1])).astype(jnp.int32).astype(jnp.int16)


def decode(ref, weight, start=0, size=None):
    rows = ref.shape[0] - PAD
    size = rows if size is None else size
    count = ref[pl.ds(rows, PAD), :].astype(jnp.float32)[0:1]
    return ref[pl.ds(start, size), :].astype(jnp.float32) * (count * weight)


def kernel(
    U, Z, H, pick, items_wide, user_wide, feedback, item_noise, user_noise, item_out, user_out, *scratch
):
    held = scratch[:H]
    zbufs = scratch[H: H + 2 * (Z - 1) * H]
    (item_rand, user_rand, nsem, user, og, arr, gs, gr, cs, cr, crd, fb, us, ur, xr, ws, wr, ug, values, sums, zsend, zrecv, isend, irecv, gsend,
     grecv, csend, crecv, cdrecv, fsem, usend, urecv, xrecv, wsend, wrecv) = scratch[H + 2 * (Z - 1) * H:]
    B, T, K = items_wide.shape
    R = T // H
    N = user.shape[0]
    G = fb.shape[1]
    groups = U // G
    piece = N // PIECES
    runs = B // RUN
    me = lax.axis_index("user")
    z = lax.axis_index("item")
    item_unit = N * FACTOR_BOUND * U / LEVELS / 32000.0
    user_unit = U * Z * T * FACTOR_BOUND * Z / LEVELS / 32000.0

    def far(axis, to, src, dst, ssem, rsem):
        return pltpu.make_async_remote_copy(
            src_ref=src, dst_ref=dst, send_sem=ssem, recv_sem=rsem,
            device_id={axis: to}, device_id_type=pl.DeviceIdType.MESH)

    barrier = pltpu.get_barrier_semaphore()

    def greet_user(j, c):
        pl.semaphore_signal(barrier, inc=1, device_id={"user": lax.rem(me + j, U)}, device_id_type=pl.DeviceIdType.MESH)
        return c

    lax.fori_loop(1, U, greet_user, 0)
    for j in range(1, Z):
        pl.semaphore_signal(barrier, inc=1, device_id={"item": lax.rem(z + j, Z)}, device_id_type=pl.DeviceIdType.MESH)

    def rows_of(h):
        return pl.ds(pl.multiple_of(lax.rem(me + h, H) * R, R), R)

    for h in range(H):
        held[h][...] = items_wide[:, rows_of(h), :].astype(jnp.bfloat16)

    pl.semaphore_wait(barrier, U - 1 + Z - 1)

    def zbuf(d, way, h):
        return held[h] if d == 0 else zbufs[(2 * (d - 1) + way) * H + h]

    def zcopy(d, way, h):
        k = (2 * (d - 1) + way) * H + h
        return far("item", z + (1 if way == 0 else -1), zbuf(d - 1, way, h), zbuf(d, way, h), zsend.at[k], zrecv.at[k])

    def can_send(d, way):
        return (z - (d - 1) >= 0) & (z + 1 < Z) if way == 0 else (z + (d - 1) < Z) & (z >= 1)

    def comes(d, way):
        return z - d >= 0 if way == 0 else z + d < Z

    for h in range(H):
        for way in (0, 1):
            pl.when(can_send(1, way))(lambda way=way, h=h: zcopy(1, way, h).start())

    user[...] = user_wide[...].astype(jnp.bfloat16)

    def slot_of(o, h):
        return o // H * H + lax.rem(o + h, H)

    def owner_of(j, h):
        return j // H * H + lax.rem(j + H - h, H)

    def icopy(p, h, to, src):
        return far("user", to, og.at[p, h, to], arr.at[p, h, slot_of(src, h)], isend.at[p, h, to], irecv.at[p, h, src])

    def spread(p, h, blocks):
        def one(j, c):
            to = lax.rem(me + j, U)
            og[p, h, to] = blocks[pick[to * Z + z, me * Z + p]]
            icopy(p, h, to, me).start()
            return c
        lax.fori_loop(1, U, one, 0)
        arr[p, h, slot_of(me, h)] = blocks[pick[me * Z + z, me * Z + p]]

    def gcopy(p, h, to, src):
        return far("user", to, gs.at[p, h, to], gr.at[p, h, src], gsend.at[p, h, to], grecv.at[p, h, src])

    def fcopy(p, g, at):
        return pltpu.make_async_copy(feedback.at[pl.ds(G * g, G), p], fb.at[at], fsem.at[at])

    lane = lax.broadcasted_iota(jnp.int32, (N, T), 1)

    def group_of(j):
        return lax.rem(me // G + groups - j, groups)

    def prefetch(p, way):
        for j in range(min(2, groups)):
            fcopy(p, group_of(j), 2 * way + j).start()

    def compute(p, h, way, send):
        def one(j, c):
            g = group_of(j)
            at = 2 * way + lax.rem(j, 2)

            def arrive(t, c):
                o = G * g + t
                pl.when(o != me)(lambda: icopy(p, h, me, o).wait_recv())
                return c

            lax.fori_loop(0, G, arrive, 0)
            fcopy(p, g, at).wait()
            tile = arr[p, h, pl.ds(G * g, G)].reshape(G * R, K)
            scores = lax.dot_general(user[...], tile, (((1,), (1,)), ((), ())), preferred_element_type=jnp.float32)
            target = []
            for m in range(G // H):
                lanes = fb[at, m * H + owner_of(H - 1, h)]
                for s in range(H - 1):
                    lanes = jnp.where((lane >= s * R) & (lane < (s + 1) * R), fb[at, m * H + owner_of(s, h)], lanes)
                target.append(lanes)
            target = jnp.concatenate(target, axis=1).astype(jnp.float32)
            residual = (0.5 * jnp.tanh(0.5 * scores) + (0.5 - target)).astype(jnp.bfloat16)
            part = lax.dot_general(residual, user[...], (((0,), (0,)), ((), ())), preferred_element_type=jnp.float32)
            for t in range(G):
                o = owner_of(G * g + t, h)
                encode(gs.at[p, h, o], part[t * R:(t + 1) * R], item_unit)

                @pl.when(o == me)
                def _():
                    gr[p, h, me] = gs[p, h, me]

                if send:
                    pl.when(o != me)(lambda: gcopy(p, h, o, me).start())
            ug[...] += jnp.dot(residual, tile, preferred_element_type=jnp.float32)
            pl.when(j + 2 < groups)(lambda: fcopy(p, group_of(j + 2), at).start())
            return c

        lax.fori_loop(0, groups, one, 0)

    def collect(p, h, way):
        def one(j, c):
            u = lax.rem(me + j, U)
            pl.when(j > 0)(lambda: gcopy(p, h, me, u).wait_recv())
            values[way, u] = decode(gr.at[p, h, u], item_unit)
            return c
        lax.fori_loop(0, U, one, 0)

    def dense(p, b, way):
        def one(u, acc):
            weight = jnp.where(pick[u * Z + z, me * Z + p] == b, 1.0, 0.0).astype(jnp.float32)
            return acc + values[way, u] * weight
        return lax.fori_loop(0, U, one, jnp.zeros((R, K), jnp.float32), unroll=8)

    def up_copy(to, p, h, c):
        return far("item", to, cs.at[p, h, c], cr.at[p, h, c], csend.at[p, h, c], crecv.at[p, h, c])

    def last_copy(to, p, h, c):
        return far("item", to, cs.at[p, h, c], crd.at[h, c], csend.at[p, h, c], cdrecv.at[h, c])

    def phase(r, h, begin, end):
        def target(way):
            return r + way * (Z - 1 - 2 * r)

        def active(way):
            return (way == 0) & (z < r) | (way == 1) & (z > Z - 1 - r)

        def source(way):
            return (way == 0) & (z == 0) | (way == 1) & (z == Z - 1)

        def in_turn(k):
            return lax.rem(k + jnp.where(2 * z < Z - 1, 0, 1), 2)

        def gather(k, carry):
            way = in_turn(k)
            pl.when(active(way))(lambda: collect(target(way), h, way))
            return carry
        lax.fori_loop(begin, end, gather, 0)

        def pass_on(c, way):
            p = target(way)
            to = z + 1 - 2 * way
            relay = jnp.logical_not(source(way))
            pl.when(relay)(lambda: up_copy(z, p, h, c).wait_recv())

            def one(i, carry):
                at = pl.ds(pl.multiple_of(i * R, R), R)
                sums[at, :] = dense(p, c * RUN + i, way)

                @pl.when(relay)
                def _():
                    sums[at, :] += decode(cr.at[p, h, c], item_unit, pl.multiple_of(i * R, R), R)
                return carry
            lax.fori_loop(0, RUN, one, 0)
            encode(cs.at[p, h, c], sums[...], item_unit)
            last = (way == 1) & (to == p)
            pl.when(last)(lambda: last_copy(to, p, h, c).start())
            pl.when(jnp.logical_not(last))(lambda: up_copy(to, p, h, c).start())

        def one(k, carry):
            way = in_turn(k // runs)
            pl.when(active(way))(lambda: pass_on(lax.rem(k, runs), way))
            return carry
        lax.fori_loop(begin * runs, end * runs, one, 0)

    def plane(d, way):
        return z - d if way == 0 else z + d

    def own_out():
        for h in range(H):
            def one(j, c):
                gcopy(z, h, lax.rem(me + j, U), me).start()
                return c
            lax.fori_loop(1, U, one, 0)

    def arrive(s):
        for e in range(1, Z):
            for way in (0, 1):
                for f in range(H):
                    @pl.when(comes(e, way) & (s == (e - 1) * H + f))
                    def _(e=e, way=way, f=f):
                        zcopy(e, way, f).wait_recv()
                        if e + 1 < Z:
                            pl.when(can_send(e + 1, way))(lambda: zcopy(e + 1, way, f).start())
                        spread(plane(e, way), f, zbuf(e, way, f))

    with jax.named_scope("spread_own"):
        for h in range(H):
            spread(z, h, held[h])
    ug[...] = jnp.zeros_like(ug)
    item_fetch = pltpu.make_async_copy(item_noise, item_rand, nsem.at[0])
    user_fetch = pltpu.make_async_copy(user_noise, user_rand, nsem.at[1])
    item_fetch.start()
    user_fetch.start()

    with jax.named_scope("compute_own"):
        def own(h, c):
            prefetch(z, 0)
            compute(z, h, 0, False)
            pl.when(h == 0)(lambda: arrive(h))
            return c
        lax.fori_loop(0, H, own, 0)

    edge = (z == 0) | (z == Z - 1)
    farthest = jnp.maximum(z, Z - 1 - z)
    steps = (Z - 1) * H

    def step(s, carry):
        d = s // H + 1
        h = lax.rem(s, H)
        for way in (0, 1):
            pl.when(comes(d, way))(lambda way=way: prefetch(plane(d, way), way))
        with jax.named_scope("arrive"):
            arrive(s + 1)
        with jax.named_scope("compute"):
            for way in (0, 1):
                pl.when(comes(d, way))(lambda way=way: compute(plane(d, way), h, way, True))
        with jax.named_scope("own_out"):
            pl.when(jnp.logical_not(edge) & (d == farthest) & (h == H - 1))(own_out)
        with jax.named_scope("phase"):
            ready = s - jnp.where(edge, 1, 0)
            pl.when((ready >= 0) & (ready < (Z - 2) * H))(lambda: phase(ready // H + 1, lax.rem(ready, H), 0, 2))
        return carry

    lax.fori_loop(0, steps, step, 0)

    half = Z // 2
    inward = jnp.where(z < half, 1, -1)
    middle = (z == half - 1) | (z == half)

    def in_copy(to, q):
        return far("item", to, us.at[q], ur.at[q], usend.at[q], urecv.at[q])

    def cross_copy(to, q):
        return far("item", to, us.at[q], xr.at[q], usend.at[q], xrecv.at[q])

    def out_copy(src, to, q):
        return far("item", to, src.at[q], wr.at[q], wsend.at[q], wrecv.at[q])

    def rows_q(q):
        return pl.ds(pl.multiple_of(q * piece, piece), piece)

    def users_in(q, carry):
        rows = rows_q(q)

        @pl.when(jnp.logical_not(edge))
        def _():
            in_copy(z, q).wait_recv()
            ug[rows, :] += decode(ur.at[q], user_unit)
        encode(us.at[q], ug[rows, :], user_unit)
        pl.when(middle)(lambda: cross_copy(z + inward, q).start())
        pl.when(jnp.logical_not(middle))(lambda: in_copy(z + inward, q).start())
        return carry

    def set_user(rows, grad):
        held_user = user_wide[rows, :]
        user_out[rows, :] = (
            held_user - step_size * (grad + prior_weight * held_user) + noise_scale * user_rand[rows, :])

    def users_out(q, carry):
        rows = rows_q(q)

        @pl.when(middle)
        def _():
            cross_copy(z, q).wait_recv()
            encode(ws.at[q], decode(us.at[q], user_unit) + decode(xr.at[q], user_unit), user_unit)
            pl.when(jnp.logical_not(edge))(lambda: out_copy(ws, z - inward, q).start())
            set_user(rows, decode(ws.at[q], user_unit))

        @pl.when(jnp.logical_not(middle))
        def _():
            out_copy(ws, z, q).wait_recv()
            pl.when(jnp.logical_not(edge))(lambda: out_copy(wr, z - inward, q).start())
            set_user(rows, decode(wr.at[q], user_unit))
        return carry

    def users_back():
        lax.fori_loop(0, PIECES, users_out, 0)

    def last_phase(first, last, k):
        def one(h, c):
            phase(Z - 1, h, k, k + 1)
            return c
        lax.fori_loop(first, last, one, 0)

    user_fetch.wait()
    with jax.named_scope("users_in"):
        lax.fori_loop(0, PIECES, users_in, 0)
    with jax.named_scope("phase_a"):
        last_phase(0, H - 1, 0)
    with jax.named_scope("users_mid"):
        pl.when(middle)(users_back)
    with jax.named_scope("phase_b"):
        last_phase(0, H - 1, 1)
    with jax.named_scope("phase_c"):
        last_phase(H - 1, H, 0)
    pl.when(edge)(own_out)
    with jax.named_scope("phase_d"):
        last_phase(H - 1, H, 1)

    def finish(h, carry):
        collect(z, h, 0)
        rows = rows_of(h)

        def one(b, carry):
            c = b // RUN
            at = pl.multiple_of(lax.rem(b, RUN) * R, R)
            item_out[b, rows, :] = dense(z, b, 0)

            @pl.when(z > 0)
            def _():
                pl.when(lax.rem(b, RUN) == 0)(lambda: up_copy(z, z, h, c).wait_recv())
                item_out[b, rows, :] += decode(cr.at[z, h, c], item_unit, at, R)

            @pl.when(z < Z - 1)
            def _():
                pl.when(lax.rem(b, RUN) == 0)(lambda: last_copy(z, z, h, c).wait_recv())
                item_out[b, rows, :] += decode(crd.at[h, c], item_unit, at, R)
            held_item = items_wide[b, rows, :]
            item_out[b, rows, :] = (
                held_item - item_step * (item_out[b, rows, :] + prior_weight * held_item)
                + item_noise_scale * item_rand[b, rows, :])
            return carry

        lax.fori_loop(0, B, one, 0)
        return carry

    item_fetch.wait()
    with jax.named_scope("finish"):
        lax.fori_loop(0, H, finish, 0)

    with jax.named_scope("userout"):
        pl.when(jnp.logical_not(middle))(users_back)

    for d in range(1, Z):
        for way in (0, 1):
            for h in range(H):
                pl.when(can_send(d, way))(lambda d=d, way=way, h=h: zcopy(d, way, h).wait_send())

    def drain(j, c):
        to = lax.rem(me + j, U)

        def one(k, c):
            icopy(k // H, lax.rem(k, H), to, me).wait_send()
            gcopy(k // H, lax.rem(k, H), to, me).wait_send()
            return c
        return lax.fori_loop(0, Z * H, one, c)

    lax.fori_loop(1, U, drain, 0)
    for j in range(1, Z):
        to = lax.rem(z + j, Z)
        def drained(k, c):
            up_copy(z, to, k // runs, lax.rem(k, runs)).wait_send()
            return c
        lax.fori_loop(0, H * runs, drained, 0)
    for q in range(PIECES):
        in_copy(z + inward, q).wait_send()
        pl.when(jnp.logical_not(edge))(lambda q=q: out_copy(ws, z - inward, q).wait_send())


def exchange(pick, items, user, feedback, item_noise, user_noise, U, Z):
    B, T, K = items.shape
    N = user.shape[0]
    H = HALVES
    R = T // H
    G = min(U, 2 * H)
    piece = N // PIECES
    runs = B // RUN
    dma = pltpu.SemaphoreType.DMA
    i16 = jnp.int16
    bf16 = jnp.bfloat16
    vmem = pl.BlockSpec(memory_space=pltpu.VMEM)
    return pl.pallas_call(
        functools.partial(kernel, U, Z, H),
        out_shape=(jax.ShapeDtypeStruct((B, T, K), jnp.float32), jax.ShapeDtypeStruct((N, K), jnp.float32)),
        in_specs=[pl.BlockSpec(memory_space=pltpu.SMEM), vmem, vmem] + [pl.BlockSpec(memory_space=pl.ANY)] * 3,
        out_specs=(vmem, vmem),
        scratch_shapes=[pltpu.VMEM((B, R, K), bf16)] * (H * (2 * (Z - 1) + 1)) + [
            pltpu.VMEM((B, T, K), jnp.float32),
            pltpu.VMEM((N, K), jnp.float32),
            dma((2,)),
            pltpu.VMEM((N, K), bf16),
            pltpu.VMEM((Z, H, U, R, K), bf16),
            pltpu.VMEM((Z, H, U, R, K), bf16),
            pltpu.VMEM((Z, H, U, R + PAD, K), i16),
            pltpu.VMEM((Z, H, U, R + PAD, K), i16),
            pltpu.VMEM((Z, H, runs, RUN * R + PAD, K), i16),
            pltpu.VMEM((Z, H, runs, RUN * R + PAD, K), i16),
            pltpu.VMEM((H, runs, RUN * R + PAD, K), i16),
            pltpu.VMEM((4, G, N, T), bf16),
        ] + [pltpu.VMEM((PIECES, piece + PAD, K), i16)] * 5 + [
            pltpu.VMEM((N, K), jnp.float32),
            pltpu.VMEM((2, U, R, K), jnp.float32),
            pltpu.VMEM((RUN * R, K), jnp.float32),
            dma((2 * (Z - 1) * H,)), dma((2 * (Z - 1) * H,)),
            dma((Z, H, U)), dma((Z, H, U)), dma((Z, H, U)), dma((Z, H, U)),
            dma((Z, H, runs)), dma((Z, H, runs)), dma((H, runs)),
            dma((4,)),
            dma((PIECES,)), dma((PIECES,)), dma((PIECES,)), dma((PIECES,)), dma((PIECES,)),
        ],
        compiler_params=pltpu.CompilerParams(
            collective_id=0, has_side_effects=True, vmem_limit_bytes=63 * 2**20),
    )(pick, items, user, feedback, item_noise, user_noise)


def local(user_factors, item_factors, feedback, item_pick, user_noise, item_noise):
    U, Z = lax.axis_size("user"), lax.axis_size("item")
    tile, rank = feedback.shape[2], item_factors.shape[1]
    held = item_factors.shape[0] // tile
    items = item_factors.reshape(held, tile, rank)
    new_item, new_user = exchange(
        item_pick, items, user_factors, feedback.reshape(U, Z, feedback.shape[1], tile),
        item_noise.reshape(items.shape), user_noise, U, Z)
    return (new_user, new_item.reshape(item_factors.shape))


def solution(mesh):
    in_specs = (
        P("user", None),
        P(("user", "item"), None),
        P("item", "user", None),
        P(),
        P("user", None),
        P(("user", "item"), None),
    )
    out_specs = (P("user", None), P(("user", "item"), None))
    return jax.shard_map(local, mesh=mesh, in_specs=in_specs, out_specs=out_specs, check_vma=False)
```

```python
import functools
import math

import jax
import jax.numpy as jnp
from jax import lax
from jax.experimental import pallas as pl
from jax.experimental.pallas import tpu as pltpu
from jax.sharding import PartitionSpec as P

step_size = 0.01
item_step = 0.1
prior_weight = 1.0
noise_scale = math.sqrt(0.02)
item_noise_scale = math.sqrt(0.2)

FACTOR_BOUND = 1.5
LEVELS = 32766.0
HALVES = 2
RUN = 4
PAD = 8
PIECES = 4


def encode(ref, value, unit):
    rows = value.shape[0]
    largest = jnp.max(jnp.abs(value), axis=0, keepdims=True)
    count = jnp.floor(largest * (1.0 / (LEVELS * unit))) + 1.0
    inverse = 1.0 / (count * unit)
    ref[pl.ds(0, rows), :] = jnp.round(value * inverse).astype(jnp.int32).astype(jnp.int16)
    ref[pl.ds(rows, PAD), :] = jnp.broadcast_to(count, (PAD, value.shape[1])).astype(jnp.int32).astype(jnp.int16)


def decode(ref, weight, start=0, size=None):
    rows = ref.shape[0] - PAD
    size = rows if size is None else size
    count = ref[pl.ds(rows, PAD), :].astype(jnp.float32)[0:1]
    return ref[pl.ds(start, size), :].astype(jnp.float32) * (count * weight)


def kernel(
    U, Z, H, pick, items_far, user_far, feedback, item_noise, user_noise, item_home, user_home, *scratch
):
    held = scratch[:H]
    zbufs = scratch[H: H + 2 * (Z - 1) * H]
    (item_out, user_out, osem, psem, items_wide, user_wide, item_rand, user_rand, nsem, user, og, arr, gs, gr, cs, cr, crd, fb, us, ur, xr, ws, wr, ug, values, sums, zsend, zrecv, isend, irecv, gsend,
     grecv, csend, crecv, cdrecv, fsem, usend, urecv, xrecv, wsend, wrecv) = scratch[H + 2 * (Z - 1) * H:]
    B, T, K = items_far.shape
    R = T // H
    N = user.shape[0]
    G = fb.shape[1]
    groups = U // G
    piece = N // PIECES
    runs = B // RUN
    me = lax.axis_index("user")
    z = lax.axis_index("item")
    item_unit = N * FACTOR_BOUND * U / LEVELS / 32000.0
    user_unit = U * Z * T * FACTOR_BOUND * Z / LEVELS / 32000.0

    def far(axis, to, src, dst, ssem, rsem):
        return pltpu.make_async_remote_copy(
            src_ref=src, dst_ref=dst, send_sem=ssem, recv_sem=rsem,
            device_id={axis: to}, device_id_type=pl.DeviceIdType.MESH)

    barrier = pltpu.get_barrier_semaphore()
    items_fetch = pltpu.make_async_copy(items_far, items_wide, nsem.at[2])
    users_fetch = pltpu.make_async_copy(user_far, user_wide, nsem.at[3])
    items_fetch.start()
    users_fetch.start()

    def greet_user(j, c):
        pl.semaphore_signal(barrier, inc=1, device_id={"user": lax.rem(me + j, U)}, device_id_type=pl.DeviceIdType.MESH)
        return c

    lax.fori_loop(1, U, greet_user, 0)
    for j in range(1, Z):
        pl.semaphore_signal(barrier, inc=1, device_id={"item": lax.rem(z + j, Z)}, device_id_type=pl.DeviceIdType.MESH)

    def rows_of(h):
        return pl.ds(pl.multiple_of(lax.rem(me + h, H) * R, R), R)

    items_fetch.wait()
    for h in range(H):
        held[h][...] = items_wide[:, rows_of(h), :].astype(jnp.bfloat16)

    pl.semaphore_wait(barrier, U - 1 + Z - 1)

    def zbuf(d, way, h):
        return held[h] if d == 0 else zbufs[(2 * (d - 1) + way) * H + h]

    def zcopy(d, way, h):
        k = (2 * (d - 1) + way) * H + h
        return far("item", z + (1 if way == 0 else -1), zbuf(d - 1, way, h), zbuf(d, way, h), zsend.at[k], zrecv.at[k])

    def can_send(d, way):
        return (z - (d - 1) >= 0) & (z + 1 < Z) if way == 0 else (z + (d - 1) < Z) & (z >= 1)

    def comes(d, way):
        return z - d >= 0 if way == 0 else z + d < Z

    for h in range(H):
        for way in (0, 1):
            pl.when(can_send(1, way))(lambda way=way, h=h: zcopy(1, way, h).start())

    users_fetch.wait()
    user[...] = user_wide[...].astype(jnp.bfloat16)

    def slot_of(o, h):
        return o // H * H + lax.rem(o + h, H)

    def owner_of(j, h):
        return j // H * H + lax.rem(j + H - h, H)

    def icopy(p, h, to, src):
        return far("user", to, og.at[p, h, to], arr.at[p, h, slot_of(src, h)], isend.at[p, h, to], irecv.at[p, h, src])

    def spread(p, h, blocks):
        def one(j, c):
            to = lax.rem(me + j, U)
            og[p, h, to] = blocks[pick[to * Z + z, me * Z + p]]
            icopy(p, h, to, me).start()
            return c
        lax.fori_loop(1, U, one, 0)
        arr[p, h, slot_of(me, h)] = blocks[pick[me * Z + z, me * Z + p]]

    def gcopy(p, h, to, src):
        return far("user", to, gs.at[p, h, to], gr.at[p, h, src], gsend.at[p, h, to], grecv.at[p, h, src])

    def fcopy(p, g, at):
        return pltpu.make_async_copy(feedback.at[pl.ds(G * g, G), p], fb.at[at], fsem.at[at])

    lane = lax.broadcasted_iota(jnp.int32, (N, T), 1)

    def group_of(j):
        return lax.rem(me // G + groups - j, groups)

    def prefetch(p, way):
        for j in range(min(2, groups)):
            fcopy(p, group_of(j), 2 * way + j).start()

    def compute(p, h, way, send):
        def one(j, c):
            g = group_of(j)
            at = 2 * way + lax.rem(j, 2)

            def arrive(t, c):
                o = G * g + t
                pl.when(o != me)(lambda: icopy(p, h, me, o).wait_recv())
                return c

            lax.fori_loop(0, G, arrive, 0)
            fcopy(p, g, at).wait()
            tile = arr[p, h, pl.ds(G * g, G)].reshape(G * R, K)
            scores = lax.dot_general(user[...], tile, (((1,), (1,)), ((), ())), preferred_element_type=jnp.float32)
            target = []
            for m in range(G // H):
                lanes = fb[at, m * H + owner_of(H - 1, h)]
                for s in range(H - 1):
                    lanes = jnp.where((lane >= s * R) & (lane < (s + 1) * R), fb[at, m * H + owner_of(s, h)], lanes)
                target.append(lanes)
            target = jnp.concatenate(target, axis=1).astype(jnp.float32)
            residual = (0.5 * jnp.tanh(0.5 * scores) + (0.5 - target)).astype(jnp.bfloat16)
            part = lax.dot_general(residual, user[...], (((0,), (0,)), ((), ())), preferred_element_type=jnp.float32)
            for t in range(G):
                o = owner_of(G * g + t, h)
                encode(gs.at[p, h, o], part[t * R:(t + 1) * R], item_unit)

                @pl.when(o == me)
                def _():
                    gr[p, h, me] = gs[p, h, me]

                if send:
                    pl.when(o != me)(lambda: gcopy(p, h, o, me).start())
            ug[...] += jnp.dot(residual, tile, preferred_element_type=jnp.float32)
            pl.when(j + 2 < groups)(lambda: fcopy(p, group_of(j + 2), at).start())
            return c

        lax.fori_loop(0, groups, one, 0)

    def collect(p, h, way):
        def one(j, c):
            u = lax.rem(me + j, U)
            pl.when(j > 0)(lambda: gcopy(p, h, me, u).wait_recv())
            values[way, u] = decode(gr.at[p, h, u], item_unit)
            return c
        lax.fori_loop(0, U, one, 0)

    def dense(p, b, way):
        def one(u, acc):
            weight = jnp.where(pick[u * Z + z, me * Z + p] == b, 1.0, 0.0).astype(jnp.float32)
            return acc + values[way, u] * weight
        return lax.fori_loop(0, U, one, jnp.zeros((R, K), jnp.float32), unroll=8)

    def up_copy(to, p, h, c):
        return far("item", to, cs.at[p, h, c], cr.at[p, h, c], csend.at[p, h, c], crecv.at[p, h, c])

    def last_copy(to, p, h, c):
        return far("item", to, cs.at[p, h, c], crd.at[h, c], csend.at[p, h, c], cdrecv.at[h, c])

    def target(r, way):
        return r + way * (Z - 1 - 2 * r)

    def active(r, way):
        return (way == 0) & (z < r) | (way == 1) & (z > Z - 1 - r)

    def in_turn(k):
        return lax.rem(k + jnp.where(2 * z < Z - 1, 0, 1), 2)

    def gather(r, h, k, bank):
        way = in_turn(k)
        pl.when(active(r, way))(lambda: collect(target(r, way), h, 2 * bank + way))

    def pass_on(r, h, k, c, bank):
        way = in_turn(k)

        @pl.when(active(r, way))
        def _():
            p = target(r, way)
            to = z + 1 - 2 * way
            relay = (way == 0) & (z > 0) | (way == 1) & (z < Z - 1)
            pl.when(relay)(lambda: up_copy(z, p, h, c).wait_recv())

            def one(i, carry):
                at = pl.ds(pl.multiple_of(i * R, R), R)
                sums[at, :] = dense(p, c * RUN + i, 2 * bank + way)

                @pl.when(relay)
                def _():
                    sums[at, :] += decode(cr.at[p, h, c], item_unit, pl.multiple_of(i * R, R), R)
                return carry
            lax.fori_loop(0, RUN, one, 0)
            encode(cs.at[p, h, c], sums[...], item_unit)
            last = (way == 1) & (to == p)
            pl.when(last)(lambda: last_copy(to, p, h, c).start())
            pl.when(jnp.logical_not(last))(lambda: up_copy(to, p, h, c).start())

    def phase(r, h):
        for k in range(2):
            gather(r, h, k, 0)

        def one(i, carry):
            pass_on(r, h, i // runs, lax.rem(i, runs), 0)
            return carry
        lax.fori_loop(0, 2 * runs, one, 0)

    def plane(d, way):
        return z - d if way == 0 else z + d

    def own_out():
        for h in range(H):
            def one(j, c):
                gcopy(z, h, lax.rem(me + j, U), me).start()
                return c
            lax.fori_loop(1, U, one, 0)

    def arrive(s):
        for e in range(1, Z):
            for way in (0, 1):
                for f in range(H):
                    @pl.when(comes(e, way) & (s == (e - 1) * H + f))
                    def _(e=e, way=way, f=f):
                        zcopy(e, way, f).wait_recv()
                        if e + 1 < Z:
                            pl.when(can_send(e + 1, way))(lambda: zcopy(e + 1, way, f).start())
                        spread(plane(e, way), f, zbuf(e, way, f))

    with jax.named_scope("spread_own"):
        for h in range(H):
            spread(z, h, held[h])
    ug[...] = jnp.zeros_like(ug)
    item_fetch = pltpu.make_async_copy(item_noise, item_rand, nsem.at[0])
    user_fetch = pltpu.make_async_copy(user_noise, user_rand, nsem.at[1])
    item_fetch.start()
    user_fetch.start()

    with jax.named_scope("compute_own"):
        def own(h, c):
            prefetch(z, 0)
            compute(z, h, 0, False)
            pl.when(h == 0)(lambda: arrive(h))
            return c
        lax.fori_loop(0, H, own, 0)

    edge = (z == 0) | (z == Z - 1)
    farthest = jnp.maximum(z, Z - 1 - z)
    steps = (Z - 1) * H

    def step(s, carry):
        d = s // H + 1
        h = lax.rem(s, H)
        for way in (0, 1):
            pl.when(comes(d, way))(lambda way=way: prefetch(plane(d, way), way))
        with jax.named_scope("arrive"):
            arrive(s + 1)
        with jax.named_scope("compute"):
            for way in (0, 1):
                pl.when(comes(d, way))(lambda way=way: compute(plane(d, way), h, way, True))
        with jax.named_scope("own_out"):
            pl.when(jnp.logical_not(edge) & (d == farthest) & (h == H - 1))(own_out)
        with jax.named_scope("phase"):
            ready = s - jnp.where(edge, 1, 0)
            pl.when((ready >= 0) & (ready < (Z - 2) * H))(lambda: phase(ready // H + 1, lax.rem(ready, H)))
        return carry

    lax.fori_loop(0, steps, step, 0)

    half = Z // 2
    inward = jnp.where(z < half, 1, -1)
    middle = (z == half - 1) | (z == half)

    def in_copy(to, q):
        return far("item", to, us.at[q], ur.at[q], usend.at[q], urecv.at[q])

    def cross_copy(to, q):
        return far("item", to, us.at[q], xr.at[q], usend.at[q], xrecv.at[q])

    def out_copy(src, to, q):
        return far("item", to, src.at[q], wr.at[q], wsend.at[q], wrecv.at[q])

    def rows_q(q):
        return pl.ds(pl.multiple_of(q * piece, piece), piece)

    def users_in(q, carry):
        rows = rows_q(q)

        @pl.when(jnp.logical_not(edge))
        def _():
            in_copy(z, q).wait_recv()
            ug[rows, :] += decode(ur.at[q], user_unit)
        encode(us.at[q], ug[rows, :], user_unit)
        pl.when(middle)(lambda: cross_copy(z + inward, q).start())
        pl.when(jnp.logical_not(middle))(lambda: in_copy(z + inward, q).start())
        return carry

    def user_back(q):
        return pltpu.make_async_copy(user_out.at[rows_q(q)], user_home.at[rows_q(q)], psem.at[q])

    def item_back(h, c):
        part = pl.ds(c * RUN, RUN)
        return pltpu.make_async_copy(item_out.at[part, rows_of(h)], item_home.at[part, rows_of(h)], osem.at[h, c])

    def set_user(rows, grad):
        held_user = user_wide[rows, :]
        user_out[rows, :] = (
            held_user - step_size * (grad + prior_weight * held_user) + noise_scale * user_rand[rows, :])

    def users_out(q, carry):
        rows = rows_q(q)

        @pl.when(middle)
        def _():
            cross_copy(z, q).wait_recv()
            encode(ws.at[q], decode(us.at[q], user_unit) + decode(xr.at[q], user_unit), user_unit)
            pl.when(jnp.logical_not(edge))(lambda: out_copy(ws, z - inward, q).start())
            set_user(rows, decode(ws.at[q], user_unit))
            user_back(q).start()

        @pl.when(jnp.logical_not(middle))
        def _():
            out_copy(ws, z, q).wait_recv()
            pl.when(jnp.logical_not(edge))(lambda: out_copy(wr, z - inward, q).start())
            set_user(rows, decode(wr.at[q], user_unit))
            user_back(q).start()
        return carry

    def drain_ingest():
        for d in range(1, Z):
            for way in (0, 1):
                for h in range(H):
                    pl.when(can_send(d, way))(lambda d=d, way=way, h=h: zcopy(d, way, h).wait_send())

        def drain(j, c):
            to = lax.rem(me + j, U)

            def one(k, c):
                icopy(k // H, lax.rem(k, H), to, me).wait_send()
                gcopy(k // H, lax.rem(k, H), to, me).wait_send()
                return c
            return lax.fori_loop(0, Z * H, one, c)

        lax.fori_loop(1, U, drain, 0)

    def users_back():
        lax.fori_loop(0, PIECES, users_out, 0)

    def drain_ingest():
        for d in range(1, Z):
            for way in (0, 1):
                for h in range(H):
                    pl.when(can_send(d, way))(lambda d=d, way=way, h=h: zcopy(d, way, h).wait_send())

        def drain(j, c):
            to = lax.rem(me + j, U)

            def one(k, c):
                icopy(k // H, lax.rem(k, H), to, me).wait_send()
                gcopy(k // H, lax.rem(k, H), to, me).wait_send()
                return c
            return lax.fori_loop(0, Z * H, one, c)

        lax.fori_loop(1, U, drain, 0)

    def users_back():
        lax.fori_loop(0, PIECES, users_out, 0)

    def last_phase(first, last, k):
        def one(h, c):
            phase(Z - 1, h, k, k + 1)
            return c
        lax.fori_loop(first, last, one, 0)

    user_fetch.wait()
    pl.when(jnp.logical_not(edge))(drain_ingest)
    with jax.named_scope("users_in"):
        lax.fori_loop(0, PIECES, users_in, 0)
    def last_order(i, carry):
        inside = (i >= runs) & (i < 3 * runs)
        j = i - runs
        h = jnp.where(inside, lax.rem(j, 2), i // (2 * runs))
        k = jnp.where(inside, 1 - lax.rem(j, 2), i // (2 * runs))
        c = jnp.where(inside, j // 2, lax.rem(i, runs))

        @pl.when(i == runs)
        def _():
            pl.when(middle)(users_back)
            gather(Z - 1, 0, 1, 0)
            gather(Z - 1, H - 1, 0, 1)
            gather(Z - 1, H - 1, 1, 1)
        pl.when((i == 3 * runs) & edge)(own_out)
        pass_on(Z - 1, h, k, c, h)
        return carry

    gather(Z - 1, 0, 0, 0)
    lax.fori_loop(0, 4 * runs, last_order, 0)
    pl.when(edge)(drain_ingest)

    def finish(h, carry):
        collect(z, h, 0)
        rows = rows_of(h)

        def one(b, carry):
            c = b // RUN
            at = pl.multiple_of(lax.rem(b, RUN) * R, R)
            item_out[b, rows, :] = dense(z, b, 0)

            @pl.when(z > 0)
            def _():
                pl.when(lax.rem(b, RUN) == 0)(lambda: up_copy(z, z, h, c).wait_recv())
                item_out[b, rows, :] += decode(cr.at[z, h, c], item_unit, at, R)

            @pl.when(z < Z - 1)
            def _():
                pl.when(lax.rem(b, RUN) == 0)(lambda: last_copy(z, z, h, c).wait_recv())
                item_out[b, rows, :] += decode(crd.at[h, c], item_unit, at, R)
            held_item = items_wide[b, rows, :]
            item_out[b, rows, :] = (
                held_item - item_step * (item_out[b, rows, :] + prior_weight * held_item)
                + item_noise_scale * item_rand[b, rows, :])
            pl.when(lax.rem(b, RUN) == RUN - 1)(lambda: item_back(h, c).start())
            return carry

        lax.fori_loop(0, B, one, 0)
        return carry

    item_fetch.wait()
    with jax.named_scope("finish"):
        lax.fori_loop(0, H, finish, 0)

    with jax.named_scope("userout"):
        pl.when(jnp.logical_not(middle))(users_back)

    for j in range(1, Z):
        to = lax.rem(z + j, Z)
        def drained(k, c):
            up_copy(z, to, k // runs, lax.rem(k, runs)).wait_send()
            return c
        lax.fori_loop(0, H * runs, drained, 0)
    for q in range(PIECES):
        user_back(q).wait()
    for h in range(H):
        for c in range(runs):
            item_back(h, c).wait()
    for q in range(PIECES):
        in_copy(z + inward, q).wait_send()
        pl.when(jnp.logical_not(edge))(lambda q=q: out_copy(ws, z - inward, q).wait_send())


def exchange(pick, items, user, feedback, item_noise, user_noise, U, Z):
    B, T, K = items.shape
    N = user.shape[0]
    H = HALVES
    R = T // H
    G = min(U, 2 * H)
    piece = N // PIECES
    runs = B // RUN
    dma = pltpu.SemaphoreType.DMA
    i16 = jnp.int16
    bf16 = jnp.bfloat16
    return pl.pallas_call(
        functools.partial(kernel, U, Z, H),
        out_shape=(jax.ShapeDtypeStruct((B, T, K), jnp.float32), jax.ShapeDtypeStruct((N, K), jnp.float32)),
        in_specs=[pl.BlockSpec(memory_space=pltpu.SMEM), ] + [pl.BlockSpec(memory_space=pl.ANY)] * 5,
        out_specs=(pl.BlockSpec(memory_space=pl.ANY),) * 2,
        scratch_shapes=[pltpu.VMEM((B, R, K), bf16)] * (H * (2 * (Z - 1) + 1)) + [
            pltpu.VMEM((B, T, K), jnp.float32),
            pltpu.VMEM((N, K), jnp.float32),
            dma((H, runs)),
            dma((PIECES,)),
            pltpu.VMEM((B, T, K), jnp.float32),
            pltpu.VMEM((N, K), jnp.float32),
            pltpu.VMEM((B, T, K), jnp.float32),
            pltpu.VMEM((N, K), jnp.float32),
            dma((4,)),
            pltpu.VMEM((N, K), bf16),
            pltpu.VMEM((Z, H, U, R, K), bf16),
            pltpu.VMEM((Z, H, U, R, K), bf16),
            pltpu.VMEM((Z, H, U, R + PAD, K), i16),
            pltpu.VMEM((Z, H, U, R + PAD, K), i16),
            pltpu.VMEM((Z, H, runs, RUN * R + PAD, K), i16),
            pltpu.VMEM((Z, H, runs, RUN * R + PAD, K), i16),
            pltpu.VMEM((H, runs, RUN * R + PAD, K), i16),
            pltpu.VMEM((4, G, N, T), bf16),
        ] + [pltpu.VMEM((PIECES, piece + PAD, K), i16)] * 5 + [
            pltpu.VMEM((N, K), jnp.float32),
            pltpu.VMEM((2 * H, U, R, K), jnp.float32),
            pltpu.VMEM((RUN * R, K), jnp.float32),
            dma((2 * (Z - 1) * H,)), dma((2 * (Z - 1) * H,)),
            dma((Z, H, U)), dma((Z, H, U)), dma((Z, H, U)), dma((Z, H, U)),
            dma((Z, H, runs)), dma((Z, H, runs)), dma((H, runs)),
            dma((4,)),
            dma((PIECES,)), dma((PIECES,)), dma((PIECES,)), dma((PIECES,)), dma((PIECES,)),
        ],
        compiler_params=pltpu.CompilerParams(
            collective_id=0, has_side_effects=True, vmem_limit_bytes=63 * 2**20),
    )(pick, items, user, feedback, item_noise, user_noise)


def local(user_factors, item_factors, feedback, item_pick, user_noise, item_noise):
    U, Z = lax.axis_size("user"), lax.axis_size("item")
    tile, rank = feedback.shape[2], item_factors.shape[1]
    held = item_factors.shape[0] // tile
    items = item_factors.reshape(held, tile, rank)
    new_item, new_user = exchange(
        item_pick, items, user_factors, feedback.reshape(U, Z, feedback.shape[1], tile),
        item_noise.reshape(items.shape), user_noise, U, Z)
    return (new_user, new_item.reshape(item_factors.shape))


def solution(mesh):
    in_specs = (
        P("user", None),
        P(("user", "item"), None),
        P("item", "user", None),
        P(),
        P("user", None),
        P(("user", "item"), None),
    )
    out_specs = (P("user", None), P(("user", "item"), None))
    return jax.shard_map(local, mesh=mesh, in_specs=in_specs, out_specs=out_specs, check_vma=False)
```

```python
import functools
import math

import jax
import jax.numpy as jnp
from jax import lax
from jax.experimental import pallas as pl
from jax.experimental.pallas import tpu as pltpu
from jax.sharding import PartitionSpec as P

step_size = 0.01
item_step = 0.1
prior_weight = 1.0
noise_scale = math.sqrt(0.02)
item_noise_scale = math.sqrt(0.2)

FACTOR_BOUND = 1.5
LEVELS = 32766.0
HALVES = 2
RUN = 4
PAD = 8
PIECES = 4
CUTS = 4


def encode(ref, value, unit):
    rows = value.shape[0]
    largest = jnp.max(jnp.abs(value), axis=0, keepdims=True)
    count = jnp.floor(largest * (1.0 / (LEVELS * unit))) + 1.0
    inverse = 1.0 / (count * unit)
    ref[pl.ds(0, rows), :] = jnp.round(value * inverse).astype(jnp.int32).astype(jnp.int16)
    ref[pl.ds(rows, PAD), :] = jnp.broadcast_to(count, (PAD, value.shape[1])).astype(jnp.int32).astype(jnp.int16)


def decode(ref, weight, start=0, size=None):
    rows = ref.shape[0] - PAD
    size = rows if size is None else size
    count = ref[pl.ds(rows, PAD), :].astype(jnp.float32)[0:1]
    return ref[pl.ds(start, size), :].astype(jnp.float32) * (count * weight)


def kernel(
    U, Z, H, pick, items_far, user_far, feedback, item_noise, user_noise, item_home, user_home, *scratch
):
    held = scratch[:H]
    zbufs = scratch[H: H + 2 * (Z - 1) * H]
    (item_out, user_out, osem, psem, items_wide, user_wide, item_rand, user_rand, nsem, user, og, arr, gs, gr, cs, cr, crd, fb, us, ur, xr, ws, wr, ug, values, sums, zsend, zrecv, isend, irecv, gsend,
     grecv, csend, crecv, cdrecv, fsem, usend, urecv, xrecv, wsend, wrecv) = scratch[H + 2 * (Z - 1) * H:]
    B, T, K = items_far.shape
    R = T // H
    N = user.shape[0]
    G = fb.shape[1]
    groups = U // G
    piece = N // PIECES
    runs = B // RUN
    me = lax.axis_index("user")
    z = lax.axis_index("item")
    item_unit = N * FACTOR_BOUND * U / LEVELS / 32000.0
    user_unit = U * Z * T * FACTOR_BOUND * Z / LEVELS / 32000.0

    def far(axis, to, src, dst, ssem, rsem):
        return pltpu.make_async_remote_copy(
            src_ref=src, dst_ref=dst, send_sem=ssem, recv_sem=rsem,
            device_id={axis: to}, device_id_type=pl.DeviceIdType.MESH)

    barrier = pltpu.get_barrier_semaphore()
    items_fetch = pltpu.make_async_copy(items_far, items_wide, nsem.at[2])
    users_fetch = pltpu.make_async_copy(user_far, user_wide, nsem.at[3])
    items_fetch.start()
    users_fetch.start()

    def greet_user(j, c):
        pl.semaphore_signal(barrier, inc=1, device_id={"user": lax.rem(me + j, U)}, device_id_type=pl.DeviceIdType.MESH)
        return c

    lax.fori_loop(1, U, greet_user, 0)
    for j in range(1, Z):
        pl.semaphore_signal(barrier, inc=1, device_id={"item": lax.rem(z + j, Z)}, device_id_type=pl.DeviceIdType.MESH)

    def rows_of(h):
        return pl.ds(pl.multiple_of(lax.rem(me + h, H) * R, R), R)

    items_fetch.wait()
    for h in range(H):
        held[h][...] = items_wide[:, rows_of(h), :].astype(jnp.bfloat16)

    pl.semaphore_wait(barrier, U - 1 + Z - 1)

    def zbuf(d, way, h):
        return held[h] if d == 0 else zbufs[(2 * (d - 1) + way) * H + h]

    def zcopy(d, way, h):
        k = (2 * (d - 1) + way) * H + h
        return far("item", z + (1 if way == 0 else -1), zbuf(d - 1, way, h), zbuf(d, way, h), zsend.at[k], zrecv.at[k])

    def can_send(d, way):
        return (z - (d - 1) >= 0) & (z + 1 < Z) if way == 0 else (z + (d - 1) < Z) & (z >= 1)

    def comes(d, way):
        return z - d >= 0 if way == 0 else z + d < Z

    for h in range(H):
        for way in (0, 1):
            pl.when(can_send(1, way))(lambda way=way, h=h: zcopy(1, way, h).start())

    users_fetch.wait()
    user[...] = user_wide[...].astype(jnp.bfloat16)

    def slot_of(o, h):
        return o // H * H + lax.rem(o + h, H)

    def owner_of(j, h):
        return j // H * H + lax.rem(j + H - h, H)

    def icopy(p, h, to, src):
        return far("user", to, og.at[p, h, to], arr.at[p, h, slot_of(src, h)], isend.at[p, h, to], irecv.at[p, h, src])

    def spread(p, h, blocks):
        def one(j, c):
            to = lax.rem(me + j, U)
            og[p, h, to] = blocks[pick[to * Z + z, me * Z + p]]
            icopy(p, h, to, me).start()
            return c
        lax.fori_loop(1, U, one, 0)
        arr[p, h, slot_of(me, h)] = blocks[pick[me * Z + z, me * Z + p]]

    def gcopy(p, h, to, src):
        return far("user", to, gs.at[p, h, to], gr.at[p, h, src], gsend.at[p, h, to], grecv.at[p, h, src])

    def fcopy(p, g, at):
        return pltpu.make_async_copy(feedback.at[pl.ds(G * g, G), p], fb.at[at], fsem.at[at])

    lane = lax.broadcasted_iota(jnp.int32, (N, T), 1)

    def group_of(j):
        return lax.rem(me // G + groups - j, groups)

    def prefetch(p, way):
        for j in range(min(2, groups)):
            fcopy(p, group_of(j), 2 * way + j).start()

    def compute(p, h, way, send):
        def one(j, c):
            g = group_of(j)
            at = 2 * way + lax.rem(j, 2)

            def arrive(t, c):
                o = G * g + t
                pl.when(o != me)(lambda: icopy(p, h, me, o).wait_recv())
                return c

            lax.fori_loop(0, G, arrive, 0)
            fcopy(p, g, at).wait()
            tile = arr[p, h, pl.ds(G * g, G)].reshape(G * R, K)
            scores = lax.dot_general(user[...], tile, (((1,), (1,)), ((), ())), preferred_element_type=jnp.float32)
            target = []
            for m in range(G // H):
                lanes = fb[at, m * H + owner_of(H - 1, h)]
                for s in range(H - 1):
                    lanes = jnp.where((lane >= s * R) & (lane < (s + 1) * R), fb[at, m * H + owner_of(s, h)], lanes)
                target.append(lanes)
            target = jnp.concatenate(target, axis=1).astype(jnp.float32)
            residual = (0.5 * jnp.tanh(0.5 * scores) + (0.5 - target)).astype(jnp.bfloat16)
            part = lax.dot_general(residual, user[...], (((0,), (0,)), ((), ())), preferred_element_type=jnp.float32)
            for t in range(G):
                o = owner_of(G * g + t, h)
                encode(gs.at[p, h, o], part[t * R:(t + 1) * R], item_unit)

                @pl.when(o == me)
                def _():
                    gr[p, h, me] = gs[p, h, me]

                if send:
                    pl.when(o != me)(lambda: gcopy(p, h, o, me).start())
            ug[...] += jnp.dot(residual, tile, preferred_element_type=jnp.float32)
            pl.when(j + 2 < groups)(lambda: fcopy(p, group_of(j + 2), at).start())
            return c

        lax.fori_loop(0, groups, one, 0)

    def collect(p, h, way):
        def one(j, c):
            u = lax.rem(me + j, U)
            pl.when(j > 0)(lambda: gcopy(p, h, me, u).wait_recv())
            values[way, u] = decode(gr.at[p, h, u], item_unit)
            return c
        lax.fori_loop(0, U, one, 0)

    def dense(p, b, way):
        def one(u, acc):
            weight = jnp.where(pick[u * Z + z, me * Z + p] == b, 1.0, 0.0).astype(jnp.float32)
            return acc + values[way, u] * weight
        return lax.fori_loop(0, U, one, jnp.zeros((R, K), jnp.float32), unroll=8)

    def up_copy(to, p, h, c):
        return far("item", to, cs.at[p, h, c], cr.at[p, h, c], csend.at[p, h, c], crecv.at[p, h, c])

    def last_copy(to, p, h, c):
        return far("item", to, cs.at[p, h, c], crd.at[h, c], csend.at[p, h, c], cdrecv.at[h, c])

    def target(r, way):
        return r + way * (Z - 1 - 2 * r)

    def active(r, way):
        return (way == 0) & (z < r) | (way == 1) & (z > Z - 1 - r)

    def in_turn(k):
        return lax.rem(k + jnp.where(2 * z < Z - 1, 0, 1), 2)

    def gather(r, h, k, bank):
        way = in_turn(k)
        pl.when(active(r, way))(lambda: collect(target(r, way), h, 2 * bank + way))

    def pass_on(r, h, k, c, bank):
        way = in_turn(k)

        @pl.when(active(r, way))
        def _():
            p = target(r, way)
            to = z + 1 - 2 * way
            relay = (way == 0) & (z > 0) | (way == 1) & (z < Z - 1)
            pl.when(relay)(lambda: up_copy(z, p, h, c).wait_recv())

            def one(i, carry):
                at = pl.ds(pl.multiple_of(i * R, R), R)
                sums[at, :] = dense(p, c * RUN + i, 2 * bank + way)

                @pl.when(relay)
                def _():
                    sums[at, :] += decode(cr.at[p, h, c], item_unit, pl.multiple_of(i * R, R), R)
                return carry
            lax.fori_loop(0, RUN, one, 0)
            encode(cs.at[p, h, c], sums[...], item_unit)
            last = (way == 1) & (to == p)
            pl.when(last)(lambda: last_copy(to, p, h, c).start())
            pl.when(jnp.logical_not(last))(lambda: up_copy(to, p, h, c).start())

    def phase(r, h):
        for k in range(2):
            gather(r, h, k, 0)

        def one(i, carry):
            pass_on(r, h, i // runs, lax.rem(i, runs), 0)
            return carry
        lax.fori_loop(0, 2 * runs, one, 0)

    def plane(d, way):
        return z - d if way == 0 else z + d

    def own_out():
        for h in range(H):
            def one(j, c):
                gcopy(z, h, lax.rem(me + j, U), me).start()
                return c
            lax.fori_loop(1, U, one, 0)

    def arrive(s):
        for e in range(1, Z):
            for way in (0, 1):
                for f in range(H):
                    @pl.when(comes(e, way) & (s == (e - 1) * H + f))
                    def _(e=e, way=way, f=f):
                        zcopy(e, way, f).wait_recv()
                        if e + 1 < Z:
                            pl.when(can_send(e + 1, way))(lambda: zcopy(e + 1, way, f).start())
                        spread(plane(e, way), f, zbuf(e, way, f))

    with jax.named_scope("spread_own"):
        for h in range(H):
            spread(z, h, held[h])
    ug[...] = jnp.zeros_like(ug)
    item_fetch = pltpu.make_async_copy(item_noise, item_rand, nsem.at[0])
    user_fetch = pltpu.make_async_copy(user_noise, user_rand, nsem.at[1])
    item_fetch.start()
    user_fetch.start()

    with jax.named_scope("compute_own"):
        def own(h, c):
            prefetch(z, 0)
            compute(z, h, 0, False)
            pl.when(h == 0)(lambda: arrive(h))
            return c
        lax.fori_loop(0, H, own, 0)

    edge = (z == 0) | (z == Z - 1)
    farthest = jnp.maximum(z, Z - 1 - z)
    steps = (Z - 1) * H

    def step(s, carry):
        d = s // H + 1
        h = lax.rem(s, H)
        for way in (0, 1):
            pl.when(comes(d, way))(lambda way=way: prefetch(plane(d, way), way))
        with jax.named_scope("arrive"):
            arrive(s + 1)
        with jax.named_scope("compute"):
            for way in (0, 1):
                pl.when(comes(d, way))(lambda way=way: compute(plane(d, way), h, way, True))
        with jax.named_scope("own_out"):
            pl.when(jnp.logical_not(edge) & (d == farthest) & (h == H - 1))(own_out)
        with jax.named_scope("phase"):
            ready = s - jnp.where(edge, 1, 0)
            pl.when((ready >= 0) & (ready < (Z - 2) * H))(lambda: phase(ready // H + 1, lax.rem(ready, H)))
        return carry

    lax.fori_loop(0, steps, step, 0)

    half = Z // 2
    inward = jnp.where(z < half, 1, -1)
    middle = (z == half - 1) | (z == half)

    def in_copy(to, q):
        return far("item", to, us.at[q], ur.at[q], usend.at[q], urecv.at[q])

    def cross_copy(to, q):
        return far("item", to, us.at[q], xr.at[q], usend.at[q], xrecv.at[q])

    def out_copy(src, to, q):
        return far("item", to, src.at[q], wr.at[q], wsend.at[q], wrecv.at[q])

    def rows_q(q):
        return pl.ds(pl.multiple_of(q * piece, piece), piece)

    def users_in(q, carry):
        rows = rows_q(q)

        @pl.when(jnp.logical_not(edge))
        def _():
            in_copy(z, q).wait_recv()
            ug[rows, :] += decode(ur.at[q], user_unit)
        encode(us.at[q], ug[rows, :], user_unit)
        pl.when(middle)(lambda: cross_copy(z + inward, q).start())
        pl.when(jnp.logical_not(middle))(lambda: in_copy(z + inward, q).start())
        return carry

    def user_back(q):
        return pltpu.make_async_copy(user_out.at[rows_q(q)], user_home.at[rows_q(q)], psem.at[q])

    def item_back(h, c):
        part = pl.ds(c * RUN, RUN)
        return pltpu.make_async_copy(item_out.at[part, rows_of(h)], item_home.at[part, rows_of(h)], osem.at[h, c])

    def set_user(rows, grad):
        held_user = user_wide[rows, :]
        user_out[rows, :] = (
            held_user - step_size * (grad + prior_weight * held_user) + noise_scale * user_rand[rows, :])

    def users_out(q, carry):
        rows = rows_q(q)

        @pl.when(middle)
        def _():
            cross_copy(z, q).wait_recv()
            encode(ws.at[q], decode(us.at[q], user_unit) + decode(xr.at[q], user_unit), user_unit)
            pl.when(jnp.logical_not(edge))(lambda: out_copy(ws, z - inward, q).start())
            set_user(rows, decode(ws.at[q], user_unit))
            user_back(q).start()

        @pl.when(jnp.logical_not(middle))
        def _():
            out_copy(ws, z, q).wait_recv()
            pl.when(jnp.logical_not(edge))(lambda: out_copy(wr, z - inward, q).start())
            set_user(rows, decode(wr.at[q], user_unit))
            user_back(q).start()
        return carry

    def drain_ingest():
        for d in range(1, Z):
            for way in (0, 1):
                for h in range(H):
                    pl.when(can_send(d, way))(lambda d=d, way=way, h=h: zcopy(d, way, h).wait_send())

        def drain(j, c):
            to = lax.rem(me + j, U)

            def one(k, c):
                icopy(k // H, lax.rem(k, H), to, me).wait_send()
                gcopy(k // H, lax.rem(k, H), to, me).wait_send()
                return c
            return lax.fori_loop(0, Z * H, one, c)

        lax.fori_loop(1, U, drain, 0)

    def users_back():
        lax.fori_loop(0, PIECES, users_out, 0)

    def drain_ingest():
        for d in range(1, Z):
            for way in (0, 1):
                for h in range(H):
                    pl.when(can_send(d, way))(lambda d=d, way=way, h=h: zcopy(d, way, h).wait_send())

        def drain(j, c):
            to = lax.rem(me + j, U)

            def one(k, c):
                icopy(k // H, lax.rem(k, H), to, me).wait_send()
                gcopy(k // H, lax.rem(k, H), to, me).wait_send()
                return c
            return lax.fori_loop(0, Z * H, one, c)

        lax.fori_loop(1, U, drain, 0)

    def users_back():
        lax.fori_loop(0, PIECES, users_out, 0)

    def last_phase(first, last, k):
        def one(h, c):
            phase(Z - 1, h, k, k + 1)
            return c
        lax.fori_loop(first, last, one, 0)

    user_fetch.wait()
    pl.when(jnp.logical_not(edge))(drain_ingest)
    with jax.named_scope("users_in"):
        lax.fori_loop(0, PIECES, users_in, 0)
    def last_order(i, carry):
        inside = (i >= runs) & (i < 3 * runs)
        j = i - runs
        h = jnp.where(inside, lax.rem(j, 2), i // (2 * runs))
        k = jnp.where(inside, 1 - lax.rem(j, 2), i // (2 * runs))
        c = jnp.where(inside, j // 2, lax.rem(i, runs))

        @pl.when(i == runs)
        def _():
            pl.when(middle)(users_back)
            gather(Z - 1, 0, 1, 0)
            gather(Z - 1, H - 1, 0, 1)
            gather(Z - 1, H - 1, 1, 1)
        pl.when((i == 3 * runs) & edge)(own_out)
        pass_on(Z - 1, h, k, c, h)
        return carry

    gather(Z - 1, 0, 0, 0)
    lax.fori_loop(0, 4 * runs, last_order, 0)
    pl.when(edge)(drain_ingest)

    def finish(h, carry):
        collect(z, h, 0)
        rows = rows_of(h)

        def one(b, carry):
            c = b // RUN
            at = pl.multiple_of(lax.rem(b, RUN) * R, R)
            item_out[b, rows, :] = dense(z, b, 0)

            @pl.when(z > 0)
            def _():
                pl.when(lax.rem(b, RUN) == 0)(lambda: up_copy(z, z, h, c).wait_recv())
                item_out[b, rows, :] += decode(cr.at[z, h, c], item_unit, at, R)

            @pl.when(z < Z - 1)
            def _():
                pl.when(lax.rem(b, RUN) == 0)(lambda: last_copy(z, z, h, c).wait_recv())
                item_out[b, rows, :] += decode(crd.at[h, c], item_unit, at, R)
            held_item = items_wide[b, rows, :]
            item_out[b, rows, :] = (
                held_item - item_step * (item_out[b, rows, :] + prior_weight * held_item)
                + item_noise_scale * item_rand[b, rows, :])
            pl.when(lax.rem(b, RUN) == RUN - 1)(lambda: item_back(h, c).start())
            return carry

        lax.fori_loop(0, B, one, 0)
        return carry

    item_fetch.wait()
    with jax.named_scope("finish"):
        lax.fori_loop(0, H, finish, 0)

    with jax.named_scope("userout"):
        pl.when(jnp.logical_not(middle))(users_back)

    for j in range(1, Z):
        to = lax.rem(z + j, Z)
        def drained(k, c):
            up_copy(z, to, k // runs, lax.rem(k, runs)).wait_send()
            return c
        lax.fori_loop(0, H * runs, drained, 0)
    for q in range(PIECES):
        user_back(q).wait()
    for h in range(H):
        for c in range(runs):
            item_back(h, c).wait()
    for q in range(PIECES):
        in_copy(z + inward, q).wait_send()
        pl.when(jnp.logical_not(edge))(lambda q=q: out_copy(ws, z - inward, q).wait_send())


def exchange(pick, items, user, feedback, item_noise, user_noise, U, Z):
    B, T, K = items.shape
    N = user.shape[0]
    H = HALVES
    R = T // H
    G = min(U, 2 * H)
    piece = N // PIECES
    runs = B // RUN
    dma = pltpu.SemaphoreType.DMA
    i16 = jnp.int16
    bf16 = jnp.bfloat16
    return pl.pallas_call(
        functools.partial(kernel, U, Z, H),
        out_shape=(jax.ShapeDtypeStruct((B, T, K), jnp.float32), jax.ShapeDtypeStruct((N, K), jnp.float32)),
        in_specs=[pl.BlockSpec(memory_space=pltpu.SMEM), ] + [pl.BlockSpec(memory_space=pl.ANY)] * 5,
        out_specs=(pl.BlockSpec(memory_space=pl.ANY),) * 2,
        scratch_shapes=[pltpu.VMEM((B, R, K), bf16)] * (H * (2 * (Z - 1) + 1)) + [
            pltpu.VMEM((B, T, K), jnp.float32),
            pltpu.VMEM((N, K), jnp.float32),
            dma((H, runs)),
            dma((PIECES,)),
            pltpu.VMEM((B, T, K), jnp.float32),
            pltpu.VMEM((N, K), jnp.float32),
            pltpu.VMEM((B, T, K), jnp.float32),
            pltpu.VMEM((N, K), jnp.float32),
            dma((4,)),
            pltpu.VMEM((N, K), bf16),
            pltpu.VMEM((Z, H, U, R, K), bf16),
            pltpu.VMEM((Z, H, U, R, K), bf16),
            pltpu.VMEM((Z, H, U, R + PAD, K), i16),
            pltpu.VMEM((Z, H, U, R + PAD, K), i16),
            pltpu.VMEM((Z, H, runs, RUN * R + PAD, K), i16),
            pltpu.VMEM((Z, H, runs, RUN * R + PAD, K), i16),
            pltpu.VMEM((H, runs, RUN * R + PAD, K), i16),
            pltpu.VMEM((4, G, N, T), bf16),
        ] + [pltpu.VMEM((PIECES, piece + PAD, K), i16)] * 5 + [
            pltpu.VMEM((N, K), jnp.float32),
            pltpu.VMEM((2 * H, U, R, K), jnp.float32),
            pltpu.VMEM((RUN * R, K), jnp.float32),
            dma((2 * (Z - 1) * H,)), dma((2 * (Z - 1) * H,)),
            dma((Z, H, U)), dma((Z, H, U)), dma((Z, H, U)), dma((Z, H, U)),
            dma((Z, H, runs)), dma((Z, H, runs)), dma((H, runs)),
            dma((4,)),
            dma((PIECES,)), dma((PIECES,)), dma((PIECES,)), dma((PIECES,)), dma((PIECES,)),
        ],
        compiler_params=pltpu.CompilerParams(
            collective_id=0, has_side_effects=True, vmem_limit_bytes=63 * 2**20),
    )(pick, items, user, feedback, item_noise, user_noise)


def settle(items_in, users_in, items_out, users_out, items_held, users_held, insem, outsem):
    parts = []
    for src, held, dst in ((items_in, items_held, items_out), (users_in, users_held, users_out)):
        rows = src.shape[0] // CUTS
        parts += [(src.at[pl.ds(i * rows, rows)], held.at[pl.ds(i * rows, rows)], dst.at[pl.ds(i * rows, rows)])
                  for i in range(CUTS)]
    first = [pltpu.make_async_copy(src, held, insem.at[i]) for i, (src, held, _) in enumerate(parts)]
    second = [pltpu.make_async_copy(held, dst, outsem.at[i]) for i, (_, held, dst) in enumerate(parts)]
    for copy in first:
        copy.start()
    for copy, onward in zip(first, second):
        copy.wait()
        onward.start()
    for onward in second:
        onward.wait()


def keep(items, users):
    anywhere = pl.BlockSpec(memory_space=pl.ANY)
    return pl.pallas_call(
        settle,
        out_shape=(jax.ShapeDtypeStruct(items.shape, items.dtype), jax.ShapeDtypeStruct(users.shape, users.dtype)),
        in_specs=[anywhere] * 2,
        out_specs=(anywhere,) * 2,
        scratch_shapes=[
            pltpu.VMEM(items.shape, items.dtype), pltpu.VMEM(users.shape, users.dtype),
            pltpu.SemaphoreType.DMA((2 * CUTS,)), pltpu.SemaphoreType.DMA((2 * CUTS,)),
        ],
    )(items, users)


def local(user_factors, item_factors, feedback, item_pick, user_noise, item_noise):
    U, Z = lax.axis_size("user"), lax.axis_size("item")
    tile, rank = feedback.shape[2], item_factors.shape[1]
    held = item_factors.shape[0] // tile
    items = item_factors.reshape(held, tile, rank)
    new_item, new_user = exchange(
        item_pick, items, user_factors, feedback.reshape(U, Z, feedback.shape[1], tile),
        item_noise.reshape(items.shape), user_noise, U, Z)
    new_item, new_user = keep(new_item.reshape(item_factors.shape), new_user)
    return (new_user, new_item)


def solution(mesh):
    in_specs = (
        P("user", None),
        P(("user", "item"), None),
        P("item", "user", None),
        P(),
        P("user", None),
        P(("user", "item"), None),
    )
    out_specs = (P("user", None), P(("user", "item"), None))
    return jax.shard_map(local, mesh=mesh, in_specs=in_specs, out_specs=out_specs, check_vma=False)
```

```python
import functools
import math

import jax
import jax.numpy as jnp
from jax import lax
from jax.experimental import pallas as pl
from jax.experimental.pallas import tpu as pltpu
from jax.sharding import PartitionSpec as P

step_size = 0.01
item_step = 0.1
prior_weight = 1.0
noise_scale = math.sqrt(0.02)
item_noise_scale = math.sqrt(0.2)

FACTOR_BOUND = 1.5
LEVELS = 32766.0
HALVES = 2
RUN = 4
PAD = 8
PIECES = 4
CUTS = 4


def encode(ref, value, unit):
    rows = value.shape[0]
    largest = jnp.max(jnp.abs(value), axis=0, keepdims=True)
    count = jnp.floor(largest * (1.0 / (LEVELS * unit))) + 1.0
    inverse = 1.0 / (count * unit)
    ref[pl.ds(0, rows), :] = jnp.round(value * inverse).astype(jnp.int32).astype(jnp.int16)
    ref[pl.ds(rows, PAD), :] = jnp.broadcast_to(count, (PAD, value.shape[1])).astype(jnp.int32).astype(jnp.int16)


def decode(ref, weight, start=0, size=None):
    rows = ref.shape[0] - PAD
    size = rows if size is None else size
    count = ref[pl.ds(rows, PAD), :].astype(jnp.float32)[0:1]
    return ref[pl.ds(start, size), :].astype(jnp.float32) * (count * weight)


def kernel(
    U, Z, H, pick, items_far, user_far, feedback, item_noise, user_noise, item_home, user_home, *scratch
):
    held = scratch[:H]
    zbufs = scratch[H: H + 2 * (Z - 1) * H]
    (item_out, user_out, osem, psem, items_wide, user_wide, item_rand, user_rand, nsem, user, og, arr, gs, gr, cs, cr, crd, fb, us, ur, xr, ws, wr, ug, values, sums, zsend, zrecv, isend, irecv, gsend,
     grecv, csend, crecv, cdrecv, fsem, usend, urecv, xrecv, wsend, wrecv) = scratch[H + 2 * (Z - 1) * H:]
    B, T, K = items_far.shape
    R = T // H
    N = user.shape[0]
    G = fb.shape[1]
    groups = U // G
    piece = N // PIECES
    runs = B // RUN
    me = lax.axis_index("user")
    z = lax.axis_index("item")
    item_unit = N * FACTOR_BOUND * U / LEVELS / 32000.0
    user_unit = U * Z * T * FACTOR_BOUND * Z / LEVELS / 32000.0

    def far(axis, to, src, dst, ssem, rsem):
        return pltpu.make_async_remote_copy(
            src_ref=src, dst_ref=dst, send_sem=ssem, recv_sem=rsem,
            device_id={axis: to}, device_id_type=pl.DeviceIdType.MESH)

    barrier = pltpu.get_barrier_semaphore()
    items_fetch = pltpu.make_async_copy(items_far, items_wide, nsem.at[2])
    users_fetch = pltpu.make_async_copy(user_far, user_wide, nsem.at[3])
    items_fetch.start()
    users_fetch.start()

    def greet_user(j, c):
        pl.semaphore_signal(barrier, inc=1, device_id={"user": lax.rem(me + j, U)}, device_id_type=pl.DeviceIdType.MESH)
        return c

    lax.fori_loop(1, U, greet_user, 0)
    for j in range(1, Z):
        pl.semaphore_signal(barrier, inc=1, device_id={"item": lax.rem(z + j, Z)}, device_id_type=pl.DeviceIdType.MESH)

    def rows_of(h):
        return pl.ds(pl.multiple_of(lax.rem(me + h, H) * R, R), R)

    items_fetch.wait()
    for h in range(H):
        held[h][...] = items_wide[:, rows_of(h), :].astype(jnp.bfloat16)

    pl.semaphore_wait(barrier, U - 1 + Z - 1)

    def zbuf(d, way, h):
        return held[h] if d == 0 else zbufs[(2 * (d - 1) + way) * H + h]

    def zcopy(d, way, h):
        k = (2 * (d - 1) + way) * H + h
        return far("item", z + (1 if way == 0 else -1), zbuf(d - 1, way, h), zbuf(d, way, h), zsend.at[k], zrecv.at[k])

    def can_send(d, way):
        return (z - (d - 1) >= 0) & (z + 1 < Z) if way == 0 else (z + (d - 1) < Z) & (z >= 1)

    def comes(d, way):
        return z - d >= 0 if way == 0 else z + d < Z

    for h in range(H):
        for way in (0, 1):
            pl.when(can_send(1, way))(lambda way=way, h=h: zcopy(1, way, h).start())

    users_fetch.wait()
    user[...] = user_wide[...].astype(jnp.bfloat16)

    def slot_of(o, h):
        return o // H * H + lax.rem(o + h, H)

    def owner_of(j, h):
        return j // H * H + lax.rem(j + H - h, H)

    def icopy(p, h, to, src):
        return far("user", to, og.at[p, h, to], arr.at[p, h, slot_of(src, h)], isend, irecv.at[p, h, src])

    def spread(p, h, blocks):
        def one(j, c):
            to = lax.rem(me + j, U)
            og[p, h, to] = blocks[pick[to * Z + z, me * Z + p]]
            icopy(p, h, to, me).start()
            return c
        lax.fori_loop(1, U, one, 0)
        arr[p, h, slot_of(me, h)] = blocks[pick[me * Z + z, me * Z + p]]

    def gcopy(p, h, to, src):
        return far("user", to, gs.at[p, h, to], gr.at[p, h, src], gsend, grecv.at[p, h, src])

    def fcopy(p, g, at):
        return pltpu.make_async_copy(feedback.at[pl.ds(G * g, G), p], fb.at[at], fsem.at[at])

    lane = lax.broadcasted_iota(jnp.int32, (N, T), 1)

    def group_of(j):
        return lax.rem(me // G + groups - j, groups)

    def prefetch(p, way):
        for j in range(min(2, groups)):
            fcopy(p, group_of(j), 2 * way + j).start()

    def compute(p, h, way, send):
        def one(j, c):
            g = group_of(j)
            at = 2 * way + lax.rem(j, 2)

            def arrive(t, c):
                o = G * g + t
                pl.when(o != me)(lambda: icopy(p, h, me, o).wait_recv())
                return c

            lax.fori_loop(0, G, arrive, 0)
            fcopy(p, g, at).wait()
            tile = arr[p, h, pl.ds(G * g, G)].reshape(G * R, K)
            scores = lax.dot_general(user[...], tile, (((1,), (1,)), ((), ())), preferred_element_type=jnp.float32)
            target = []
            for m in range(G // H):
                lanes = fb[at, m * H + owner_of(H - 1, h)]
                for s in range(H - 1):
                    lanes = jnp.where((lane >= s * R) & (lane < (s + 1) * R), fb[at, m * H + owner_of(s, h)], lanes)
                target.append(lanes)
            target = jnp.concatenate(target, axis=1).astype(jnp.float32)
            residual = (0.5 * jnp.tanh(0.5 * scores) + (0.5 - target)).astype(jnp.bfloat16)
            part = lax.dot_general(residual, user[...], (((0,), (0,)), ((), ())), preferred_element_type=jnp.float32)
            for t in range(G):
                o = owner_of(G * g + t, h)
                encode(gs.at[p, h, o], part[t * R:(t + 1) * R], item_unit)

                @pl.when(o == me)
                def _():
                    gr[p, h, me] = gs[p, h, me]

                if send:
                    pl.when(o != me)(lambda: gcopy(p, h, o, me).start())
            ug[...] += jnp.dot(residual, tile, preferred_element_type=jnp.float32)
            pl.when(j + 2 < groups)(lambda: fcopy(p, group_of(j + 2), at).start())
            return c

        lax.fori_loop(0, groups, one, 0)

    def collect(p, h, way):
        def one(j, c):
            u = lax.rem(me + j, U)
            pl.when(j > 0)(lambda: gcopy(p, h, me, u).wait_recv())
            values[way, u] = decode(gr.at[p, h, u], item_unit)
            return c
        lax.fori_loop(0, U, one, 0)

    def dense(p, b, way):
        def one(u, acc):
            weight = jnp.where(pick[u * Z + z, me * Z + p] == b, 1.0, 0.0).astype(jnp.float32)
            return acc + values[way, u] * weight
        return lax.fori_loop(0, U, one, jnp.zeros((R, K), jnp.float32), unroll=8)

    def up_copy(to, p, h, c):
        return far("item", to, cs.at[p, h, c], cr.at[p, h, c], csend.at[p, h, c], crecv.at[p, h, c])

    def last_copy(to, p, h, c):
        return far("item", to, cs.at[p, h, c], crd.at[h, c], csend.at[p, h, c], cdrecv.at[h, c])

    def target(r, way):
        return r + way * (Z - 1 - 2 * r)

    def active(r, way):
        return (way == 0) & (z < r) | (way == 1) & (z > Z - 1 - r)

    def in_turn(k):
        return lax.rem(k + jnp.where(2 * z < Z - 1, 0, 1), 2)

    def gather(r, h, k, bank):
        way = in_turn(k)
        pl.when(active(r, way))(lambda: collect(target(r, way), h, 2 * bank + way))

    def pass_on(r, h, k, c, bank):
        way = in_turn(k)

        @pl.when(active(r, way))
        def _():
            p = target(r, way)
            to = z + 1 - 2 * way
            relay = (way == 0) & (z > 0) | (way == 1) & (z < Z - 1)
            pl.when(relay)(lambda: up_copy(z, p, h, c).wait_recv())

            def one(i, carry):
                at = pl.ds(pl.multiple_of(i * R, R), R)
                sums[at, :] = dense(p, c * RUN + i, 2 * bank + way)

                @pl.when(relay)
                def _():
                    sums[at, :] += decode(cr.at[p, h, c], item_unit, pl.multiple_of(i * R, R), R)
                return carry
            lax.fori_loop(0, RUN, one, 0)
            encode(cs.at[p, h, c], sums[...], item_unit)
            last = (way == 1) & (to == p)
            pl.when(last)(lambda: last_copy(to, p, h, c).start())
            pl.when(jnp.logical_not(last))(lambda: up_copy(to, p, h, c).start())

    def phase(r, h):
        for k in range(2):
            gather(r, h, k, 0)

        def one(i, carry):
            pass_on(r, h, i // runs, lax.rem(i, runs), 0)
            return carry
        lax.fori_loop(0, 2 * runs, one, 0)

    def plane(d, way):
        return z - d if way == 0 else z + d

    def own_out():
        for h in range(H):
            def one(j, c):
                gcopy(z, h, lax.rem(me + j, U), me).start()
                return c
            lax.fori_loop(1, U, one, 0)

    def arrive(s):
        for e in range(1, Z):
            for way in (0, 1):
                for f in range(H):
                    @pl.when(comes(e, way) & (s == (e - 1) * H + f))
                    def _(e=e, way=way, f=f):
                        zcopy(e, way, f).wait_recv()
                        if e + 1 < Z:
                            pl.when(can_send(e + 1, way))(lambda: zcopy(e + 1, way, f).start())
                        spread(plane(e, way), f, zbuf(e, way, f))

    with jax.named_scope("spread_own"):
        for h in range(H):
            spread(z, h, held[h])
    ug[...] = jnp.zeros_like(ug)
    item_fetch = pltpu.make_async_copy(item_noise, item_rand, nsem.at[0])
    user_fetch = pltpu.make_async_copy(user_noise, user_rand, nsem.at[1])
    item_fetch.start()
    user_fetch.start()

    with jax.named_scope("compute_own"):
        def own(h, c):
            prefetch(z, 0)
            compute(z, h, 0, False)
            pl.when(h == 0)(lambda: arrive(h))
            return c
        lax.fori_loop(0, H, own, 0)

    edge = (z == 0) | (z == Z - 1)
    farthest = jnp.maximum(z, Z - 1 - z)
    steps = (Z - 1) * H

    def step(s, carry):
        d = s // H + 1
        h = lax.rem(s, H)
        for way in (0, 1):
            pl.when(comes(d, way))(lambda way=way: prefetch(plane(d, way), way))
        with jax.named_scope("arrive"):
            arrive(s + 1)
        with jax.named_scope("compute"):
            for way in (0, 1):
                pl.when(comes(d, way))(lambda way=way: compute(plane(d, way), h, way, True))
        with jax.named_scope("own_out"):
            pl.when(jnp.logical_not(edge) & (d == farthest) & (h == H - 1))(own_out)
        with jax.named_scope("phase"):
            ready = s - jnp.where(edge, 1, 0)
            pl.when((ready >= 0) & (ready < (Z - 2) * H))(lambda: phase(ready // H + 1, lax.rem(ready, H)))
        return carry

    lax.fori_loop(0, steps, step, 0)

    half = Z // 2
    inward = jnp.where(z < half, 1, -1)
    middle = (z == half - 1) | (z == half)

    def in_copy(to, q):
        return far("item", to, us.at[q], ur.at[q], usend.at[q], urecv.at[q])

    def cross_copy(to, q):
        return far("item", to, us.at[q], xr.at[q], usend.at[q], xrecv.at[q])

    def out_copy(src, to, q):
        return far("item", to, src.at[q], wr.at[q], wsend.at[q], wrecv.at[q])

    def rows_q(q):
        return pl.ds(pl.multiple_of(q * piece, piece), piece)

    def users_in(q, carry):
        rows = rows_q(q)

        @pl.when(jnp.logical_not(edge))
        def _():
            in_copy(z, q).wait_recv()
            ug[rows, :] += decode(ur.at[q], user_unit)
        encode(us.at[q], ug[rows, :], user_unit)
        pl.when(middle)(lambda: cross_copy(z + inward, q).start())
        pl.when(jnp.logical_not(middle))(lambda: in_copy(z + inward, q).start())
        return carry

    def user_back(q):
        return pltpu.make_async_copy(user_out.at[rows_q(q)], user_home.at[rows_q(q)], psem.at[q])

    def item_back(h, c):
        part = pl.ds(c * RUN, RUN)
        return pltpu.make_async_copy(item_out.at[part, rows_of(h)], item_home.at[part, rows_of(h)], osem.at[h, c])

    def set_user(rows, grad):
        held_user = user_wide[rows, :]
        user_out[rows, :] = (
            held_user - step_size * (grad + prior_weight * held_user) + noise_scale * user_rand[rows, :])

    def users_out(q, carry):
        rows = rows_q(q)

        @pl.when(middle)
        def _():
            cross_copy(z, q).wait_recv()
            encode(ws.at[q], decode(us.at[q], user_unit) + decode(xr.at[q], user_unit), user_unit)
            pl.when(jnp.logical_not(edge))(lambda: out_copy(ws, z - inward, q).start())
            set_user(rows, decode(ws.at[q], user_unit))
            user_back(q).start()

        @pl.when(jnp.logical_not(middle))
        def _():
            out_copy(ws, z, q).wait_recv()
            pl.when(jnp.logical_not(edge))(lambda: out_copy(wr, z - inward, q).start())
            set_user(rows, decode(wr.at[q], user_unit))
            user_back(q).start()
        return carry

    def drain_ingest():
        for d in range(1, Z):
            for way in (0, 1):
                for h in range(H):
                    pl.when(can_send(d, way))(lambda d=d, way=way, h=h: zcopy(d, way, h).wait_send())

        others = pl.ds(0, U - 1)
        pltpu.make_async_copy(og.at[:, :, others], og.at[:, :, others], isend).wait()
        pltpu.make_async_copy(gs.at[:, :, others], gs.at[:, :, others], gsend).wait()

    def users_back():
        lax.fori_loop(0, PIECES, users_out, 0)

    def drain_ingest():
        for d in range(1, Z):
            for way in (0, 1):
                for h in range(H):
                    pl.when(can_send(d, way))(lambda d=d, way=way, h=h: zcopy(d, way, h).wait_send())

        others = pl.ds(0, U - 1)
        pltpu.make_async_copy(og.at[:, :, others], og.at[:, :, others], isend).wait()
        pltpu.make_async_copy(gs.at[:, :, others], gs.at[:, :, others], gsend).wait()

    def users_back():
        lax.fori_loop(0, PIECES, users_out, 0)

    def last_phase(first, last, k):
        def one(h, c):
            phase(Z - 1, h, k, k + 1)
            return c
        lax.fori_loop(first, last, one, 0)

    user_fetch.wait()
    pl.when(jnp.logical_not(edge))(drain_ingest)
    with jax.named_scope("users_in"):
        lax.fori_loop(0, PIECES, users_in, 0)
    def last_order(i, carry):
        inside = (i >= runs) & (i < 3 * runs)
        j = i - runs
        h = jnp.where(inside, lax.rem(j, 2), i // (2 * runs))
        k = jnp.where(inside, 1 - lax.rem(j, 2), i // (2 * runs))
        c = jnp.where(inside, j // 2, lax.rem(i, runs))

        @pl.when(i == runs)
        def _():
            pl.when(middle)(users_back)
            gather(Z - 1, 0, 1, 0)
            gather(Z - 1, H - 1, 0, 1)
            gather(Z - 1, H - 1, 1, 1)
        pl.when((i == 3 * runs) & edge)(own_out)
        pass_on(Z - 1, h, k, c, h)
        return carry

    gather(Z - 1, 0, 0, 0)
    lax.fori_loop(0, 4 * runs, last_order, 0)
    pl.when(edge)(drain_ingest)

    def finish(h, carry):
        collect(z, h, 0)
        rows = rows_of(h)

        def one(b, carry):
            c = b // RUN
            at = pl.multiple_of(lax.rem(b, RUN) * R, R)
            item_out[b, rows, :] = dense(z, b, 0)

            @pl.when(z > 0)
            def _():
                pl.when(lax.rem(b, RUN) == 0)(lambda: up_copy(z, z, h, c).wait_recv())
                item_out[b, rows, :] += decode(cr.at[z, h, c], item_unit, at, R)

            @pl.when(z < Z - 1)
            def _():
                pl.when(lax.rem(b, RUN) == 0)(lambda: last_copy(z, z, h, c).wait_recv())
                item_out[b, rows, :] += decode(crd.at[h, c], item_unit, at, R)
            held_item = items_wide[b, rows, :]
            item_out[b, rows, :] = (
                held_item - item_step * (item_out[b, rows, :] + prior_weight * held_item)
                + item_noise_scale * item_rand[b, rows, :])
            pl.when(lax.rem(b, RUN) == RUN - 1)(lambda: item_back(h, c).start())
            return carry

        lax.fori_loop(0, B, one, 0)
        return carry

    item_fetch.wait()
    with jax.named_scope("finish"):
        lax.fori_loop(0, H, finish, 0)

    with jax.named_scope("userout"):
        pl.when(jnp.logical_not(middle))(users_back)

    for j in range(1, Z):
        to = lax.rem(z + j, Z)
        def drained(k, c):
            up_copy(z, to, k // runs, lax.rem(k, runs)).wait_send()
            return c
        lax.fori_loop(0, H * runs, drained, 0)
    for q in range(PIECES):
        user_back(q).wait()
    for h in range(H):
        for c in range(runs):
            item_back(h, c).wait()
    for q in range(PIECES):
        in_copy(z + inward, q).wait_send()
        pl.when(jnp.logical_not(edge))(lambda q=q: out_copy(ws, z - inward, q).wait_send())


def exchange(pick, items, user, feedback, item_noise, user_noise, U, Z):
    B, T, K = items.shape
    N = user.shape[0]
    H = HALVES
    R = T // H
    G = min(U, 2 * H)
    piece = N // PIECES
    runs = B // RUN
    dma = pltpu.SemaphoreType.DMA
    i16 = jnp.int16
    bf16 = jnp.bfloat16
    return pl.pallas_call(
        functools.partial(kernel, U, Z, H),
        out_shape=(jax.ShapeDtypeStruct((B, T, K), jnp.float32), jax.ShapeDtypeStruct((N, K), jnp.float32)),
        in_specs=[pl.BlockSpec(memory_space=pltpu.SMEM), ] + [pl.BlockSpec(memory_space=pl.ANY)] * 5,
        out_specs=(pl.BlockSpec(memory_space=pl.ANY),) * 2,
        scratch_shapes=[pltpu.VMEM((B, R, K), bf16)] * (H * (2 * (Z - 1) + 1)) + [
            pltpu.VMEM((B, T, K), jnp.float32),
            pltpu.VMEM((N, K), jnp.float32),
            dma((H, runs)),
            dma((PIECES,)),
            pltpu.VMEM((B, T, K), jnp.float32),
            pltpu.VMEM((N, K), jnp.float32),
            pltpu.VMEM((B, T, K), jnp.float32),
            pltpu.VMEM((N, K), jnp.float32),
            dma((4,)),
            pltpu.VMEM((N, K), bf16),
            pltpu.VMEM((Z, H, U, R, K), bf16),
            pltpu.VMEM((Z, H, U, R, K), bf16),
            pltpu.VMEM((Z, H, U, R + PAD, K), i16),
            pltpu.VMEM((Z, H, U, R + PAD, K), i16),
            pltpu.VMEM((Z, H, runs, RUN * R + PAD, K), i16),
            pltpu.VMEM((Z, H, runs, RUN * R + PAD, K), i16),
            pltpu.VMEM((H, runs, RUN * R + PAD, K), i16),
            pltpu.VMEM((4, G, N, T), bf16),
        ] + [pltpu.VMEM((PIECES, piece + PAD, K), i16)] * 5 + [
            pltpu.VMEM((N, K), jnp.float32),
            pltpu.VMEM((2 * H, U, R, K), jnp.float32),
            pltpu.VMEM((RUN * R, K), jnp.float32),
            dma((2 * (Z - 1) * H,)), dma((2 * (Z - 1) * H,)),
            dma, dma((Z, H, U)), dma, dma((Z, H, U)),
            dma((Z, H, runs)), dma((Z, H, runs)), dma((H, runs)),
            dma((4,)),
            dma((PIECES,)), dma((PIECES,)), dma((PIECES,)), dma((PIECES,)), dma((PIECES,)),
        ],
        compiler_params=pltpu.CompilerParams(
            collective_id=0, has_side_effects=True, vmem_limit_bytes=63 * 2**20),
    )(pick, items, user, feedback, item_noise, user_noise)


def settle(items_in, users_in, items_out, users_out, items_held, users_held, insem, outsem):
    parts = []
    for src, held, dst in ((items_in, items_held, items_out), (users_in, users_held, users_out)):
        rows = src.shape[0] // CUTS
        parts += [(src.at[pl.ds(i * rows, rows)], held.at[pl.ds(i * rows, rows)], dst.at[pl.ds(i * rows, rows)])
                  for i in range(CUTS)]
    first = [pltpu.make_async_copy(src, held, insem.at[i]) for i, (src, held, _) in enumerate(parts)]
    second = [pltpu.make_async_copy(held, dst, outsem.at[i]) for i, (_, held, dst) in enumerate(parts)]
    for copy in first:
        copy.start()
    for copy, onward in zip(first, second):
        copy.wait()
        onward.start()
    for onward in second:
        onward.wait()


def keep(items, users):
    anywhere = pl.BlockSpec(memory_space=pl.ANY)
    return pl.pallas_call(
        settle,
        out_shape=(jax.ShapeDtypeStruct(items.shape, items.dtype), jax.ShapeDtypeStruct(users.shape, users.dtype)),
        in_specs=[anywhere] * 2,
        out_specs=(anywhere,) * 2,
        scratch_shapes=[
            pltpu.VMEM(items.shape, items.dtype), pltpu.VMEM(users.shape, users.dtype),
            pltpu.SemaphoreType.DMA((2 * CUTS,)), pltpu.SemaphoreType.DMA((2 * CUTS,)),
        ],
    )(items, users)


def local(user_factors, item_factors, feedback, item_pick, user_noise, item_noise):
    U, Z = lax.axis_size("user"), lax.axis_size("item")
    tile, rank = feedback.shape[2], item_factors.shape[1]
    held = item_factors.shape[0] // tile
    items = item_factors.reshape(held, tile, rank)
    new_item, new_user = exchange(
        item_pick, items, user_factors, feedback.reshape(U, Z, feedback.shape[1], tile),
        item_noise.reshape(items.shape), user_noise, U, Z)
    new_item, new_user = keep(new_item.reshape(item_factors.shape), new_user)
    return (new_user, new_item)


def solution(mesh):
    in_specs = (
        P("user", None),
        P(("user", "item"), None),
        P("item", "user", None),
        P(),
        P("user", None),
        P(("user", "item"), None),
    )
    out_specs = (P("user", None), P(("user", "item"), None))
    return jax.shard_map(local, mesh=mesh, in_specs=in_specs, out_specs=out_specs, check_vma=False)
```
